256 devices in a mesh: tok: 64 (over y, z, core), head: 4 (over x).
Axes of the slice: x: 4, y: 4, z: 8, core: 2. Of those that a mesh axis runs over, the one named last changes fastest.
Arguments:
- query_rows: bfloat16 [32768, 4, 1024], P('tok', 'head'), may hold values from -6 to 6
- key_rows: bfloat16 [32768, 4, 128], P('tok', 'head'), may hold values from -6 to 6
- value_rows: bfloat16 [32768, 4, 128], P('tok', 'head'), may hold values from -6 to 6
- output_gradient: bfloat16 [32768, 4, 1024], P('tok', 'head'), may hold values from -6 to 6
- row_logsumexp: bfloat16 [4, 8, 32768], P('head', None, 'tok'), may hold values from 3 to 7
- row_delta_sums: bfloat16 [4, 8, 32768], P('head', None, 'tok'), may hold values from -5 to 5
- segments: int32 [32768], replicated, may hold values from 0 to 32767, as said below
- query_key_value_weight: bfloat16 [4096, 4, 1280], P('tok', 'head'), may hold values from -0.09375 to 0.09375
Outputs:
- grad_input: bfloat16 [32768, 4096], P('tok', 'head')
The draws below stay inside these ranges and needn't reach their ends.
Inputs may be any that keep to these rules, and one draw needn't show every extreme that they name: `segments`: numbers never fall along the tokens, and every document lies inside one window of 512 consecutive tokens.
All inputs are finite; a program needn't handle non-finite values.
Results may differ from the reference program's by a relative error of at most 0.012.
Values may be sent and summed in bfloat16 or wider, within the bound.
No kernel may reach another device: no remote copies, remote signals or barrier semaphores. Data moves between devices by JAX's collectives and lax.ppermute only.
A program may use at most 128 MiB of HBM per device.

```python
import jax
import jax.numpy as jnp
from jax import lax

MODEL_WIDTH = 4096
QUERY_HEADS = 32
KEY_VALUE_HEADS = 4
HEAD_WIDTH = 128
BLOCK = 128
WINDOW_TOKENS = 512
GROUP_KV_HEADS = 1
TOKEN_TOTAL = 32768
N_TOK = 64


def document_plan(key):
    windows = TOKEN_TOTAL // WINDOW_TOKENS
    half_axis = windows // 2
    window_ids = jnp.arange(windows, dtype=jnp.int32)
    positions = jnp.arange(WINDOW_TOKENS, dtype=jnp.int32)
    sparse_density = jax.random.randint(jax.random.fold_in(key, 11), (windows, 1), 0, 2)
    dense_density = jax.random.randint(jax.random.fold_in(key, 13), (windows, 1), 64, 193)
    density = jnp.where(window_ids[:, None] < half_axis, sparse_density, dense_density)
    rolls = jax.random.randint(jax.random.fold_in(key, 12), (windows, WINDOW_TOKENS), 0, 64 * BLOCK)
    cut_flags = (rolls < density) & (positions[None, :] > 0)
    block_cuts = (positions % BLOCK == 0) & (positions > 0)
    cut_flags = jnp.where(window_ids[:, None] == 0, False, cut_flags)
    cut_flags = jnp.where(window_ids[:, None] == half_axis, block_cuts[None, :], cut_flags)
    local_ids = jnp.cumsum(cut_flags.astype(jnp.int32), axis=1)
    return local_ids + window_ids[:, None] * WINDOW_TOKENS


def draw_segments(key, part):
    return document_plan(key).reshape(TOKEN_TOTAL).astype(jnp.int32)


def levels(stream_key, dims, split, smallest, top_value):
    factor_of, own = 1.0, jax.random.fold_in(stream_key, 6)
    for position, shards_of in split:
        heights = jnp.exp(jax.random.uniform(jax.random.fold_in(own, position), (shards_of,), jnp.float32, smallest / len(split), top_value / len(split)))
        factor_of = factor_of * jnp.repeat(heights, dims[position] // shards_of).reshape([-1 if axis == position else 1 for axis in range(len(dims))])
    return factor_of


def scatter_about(rng, dims, deviation, most, shards=(), held_as=jnp.bfloat16):
    loudness = levels(rng, dims, shards, -0.22, 0.18) if shards else 1.0
    array = jax.random.normal(rng, dims, jnp.float32) * deviation * loudness
    return jnp.minimum(jnp.maximum(array, -most), most).astype(held_as)


def setup_inputs(seed: int = 0) -> dict:
    keys = jax.random.split(jax.random.key(seed), 9)
    return {
        "query_rows": scatter_about(keys[0], (TOKEN_TOTAL, KEY_VALUE_HEADS, QUERY_HEADS // KEY_VALUE_HEADS * HEAD_WIDTH), 1.0, 6.0, ((0, 64), (1, 4))),
        "key_rows": scatter_about(keys[1], (TOKEN_TOTAL, KEY_VALUE_HEADS, HEAD_WIDTH), 1.0, 6.0, ((0, 64), (1, 4))),
        "value_rows": scatter_about(keys[2], (TOKEN_TOTAL, KEY_VALUE_HEADS, HEAD_WIDTH), 1.0, 6.0, ((0, 64), (1, 4))),
        "output_gradient": scatter_about(keys[3], (TOKEN_TOTAL, KEY_VALUE_HEADS, QUERY_HEADS // KEY_VALUE_HEADS * HEAD_WIDTH), 1.0, 6.0, ((0, 64), (1, 4))),
        "row_logsumexp": jnp.clip(3.0 + 4.0 * jax.random.uniform(keys[4], (KEY_VALUE_HEADS, QUERY_HEADS // KEY_VALUE_HEADS, TOKEN_TOTAL), jnp.float32) ** levels(keys[4], (KEY_VALUE_HEADS, QUERY_HEADS // KEY_VALUE_HEADS, TOKEN_TOTAL), ((0, 4), (2, 64)), -0.2, 0.2), 3.0, 7.0).astype(jnp.bfloat16),
        "row_delta_sums": scatter_about(keys[5], (KEY_VALUE_HEADS, QUERY_HEADS // KEY_VALUE_HEADS, TOKEN_TOTAL), 1.0, 5.0, ((0, 4), (2, 64))),
        "segments": draw_segments(jax.random.fold_in(keys[8], 71), 0),
        "query_key_value_weight": scatter_about(keys[7], (MODEL_WIDTH, KEY_VALUE_HEADS, (QUERY_HEADS // KEY_VALUE_HEADS + 2) * HEAD_WIDTH), MODEL_WIDTH ** -0.5, 0.09375, ((0, 64), (1, 4))),
    }


def reference(query_rows, key_rows, value_rows, output_gradient, row_logsumexp, row_delta_sums, segments, query_key_value_weight):
    heads_per_group = QUERY_HEADS // KEY_VALUE_HEADS
    score_scale = HEAD_WIDTH ** -0.5
    offsets = jnp.arange(WINDOW_TOKENS)
    causal = offsets[None, :] <= offsets[:, None]

    def one_window(window_index):
        leading_row = (window_index * WINDOW_TOKENS).astype(jnp.int32)
        query_window_rows = lax.dynamic_slice_in_dim(query_rows, leading_row, WINDOW_TOKENS, 0).astype(jnp.float32).reshape(WINDOW_TOKENS, KEY_VALUE_HEADS, heads_per_group, HEAD_WIDTH)
        output_grad_window = lax.dynamic_slice_in_dim(output_gradient, leading_row, WINDOW_TOKENS, 0).astype(jnp.float32).reshape(WINDOW_TOKENS, KEY_VALUE_HEADS, heads_per_group, HEAD_WIDTH)
        key_win = lax.dynamic_slice_in_dim(key_rows, leading_row, WINDOW_TOKENS, 0).astype(jnp.float32)
        value_win = lax.dynamic_slice_in_dim(value_rows, leading_row, WINDOW_TOKENS, 0).astype(jnp.float32)
        lse_win = lax.dynamic_slice_in_dim(row_logsumexp, leading_row, WINDOW_TOKENS, 2).astype(jnp.float32)
        delta_win = lax.dynamic_slice_in_dim(row_delta_sums, leading_row, WINDOW_TOKENS, 2).astype(jnp.float32)
        seg_win = lax.dynamic_slice_in_dim(segments, leading_row, WINDOW_TOKENS, 0)
        allowed = (seg_win[:, None] == seg_win[None, :]) & causal
        scores = jnp.einsum("agrd,bgd->grab", query_window_rows, key_win) * score_scale
        soft_probs = jnp.where(allowed[None, None], jnp.exp(scores - lse_win[..., None]), 0.0)
        probs_low = lax.optimization_barrier(soft_probs.astype(jnp.bfloat16)).astype(jnp.float32)
        value_gradient = jnp.einsum("grab,agrd->bgd", probs_low, output_grad_window)
        grad_prob = jnp.einsum("agrd,bgd->grab", output_grad_window, value_win)
        grad_score = soft_probs * (grad_prob - delta_win[..., None])
        score_low = lax.optimization_barrier(grad_score.astype(jnp.bfloat16)).astype(jnp.float32)
        query_gradient = jnp.einsum("grab,bgd->agrd", score_low, key_win) * score_scale
        key_gradient = jnp.einsum("grab,agrd->bgd", score_low, query_window_rows) * score_scale
        stacked_gradients = jnp.concatenate([query_gradient.reshape(WINDOW_TOKENS, KEY_VALUE_HEADS, heads_per_group * HEAD_WIDTH), key_gradient, value_gradient], axis=2).astype(jnp.bfloat16)
        running_sum = jnp.zeros((WINDOW_TOKENS, MODEL_WIDTH), jnp.float32)
        for group_of_heads in range(KEY_VALUE_HEADS // GROUP_KV_HEADS):
            first_head = group_of_heads * GROUP_KV_HEADS
            part_rows = stacked_gradients[:, first_head:first_head + GROUP_KV_HEADS, :].reshape(WINDOW_TOKENS, -1)
            part_weights = query_key_value_weight[:, first_head:first_head + GROUP_KV_HEADS, :].reshape(MODEL_WIDTH, -1)
            group_term = jnp.dot(part_rows, part_weights.T, preferred_element_type=jnp.float32)
            running_sum = running_sum + lax.optimization_barrier(group_term.astype(jnp.bfloat16)).astype(jnp.float32)
        return running_sum.astype(jnp.bfloat16)

    return lax.map(one_window, jnp.arange(N_TOK, dtype=jnp.int32)).reshape(TOKEN_TOTAL, MODEL_WIDTH)
```

```python
import jax
import jax.numpy as jnp
import numpy as np
from jax import lax
from jax.experimental import pallas as pl
from jax.experimental.pallas import tpu as pltpu
from jax.sharding import Mesh, PartitionSpec as P

SIZES = {"y": 4, "z": 8, "c": 2, "x": 4}
BLOCK = 128
MASKED = -1e30
LOG2E = 1.4426950408889634


def move(value, axes, target):
    dims = [SIZES[a] for a in axes]
    pairs = []
    for source in range(int(np.prod(dims))):
        coords = dict(zip(axes, (int(v) for v in np.unravel_index(source, dims))))
        goal = target(**coords)
        goal = [goal[a] % SIZES[a] for a in axes]
        pairs.append((source, int(np.ravel_multi_index(goal, dims))))
    return lax.ppermute(value, axes, pairs)


def swap_cores(value):
    return move(value, ("c",), lambda c: dict(c=1 - c))


def along(value, axis, steps):
    sign = lambda c: steps if c == 0 else -steps
    return move(value, (axis, "c"), lambda c, **k: {axis: k[axis] + sign(c), "c": c})


def shift(value, axis, steps):
    return move(value, (axis,), lambda **k: {axis: k[axis] + steps})


def nt(a, b):
    return lax.dot_general(a, b, (((1,), (1,)), ((), ())), preferred_element_type=jnp.float32)


def nn(a, b):
    return jnp.dot(a, b, preferred_element_type=jnp.float32)


def attention_kernel(q_ref, do_ref, k_ref, v_ref, lse_ref, delta_ref, seg_ref, out_ref,
                     bias, key_t, lse_f, delta_f, dk_acc, dv_acc):
    head = pl.program_id(0)
    heads = pl.num_programs(0)
    window, size = k_ref.shape
    scale = size ** -0.5

    @pl.when(head == 0)
    def _():
        lse_f[...] = lse_ref[...].astype(jnp.float32) * LOG2E
        delta_f[...] = delta_ref[...].astype(jnp.float32)
        key_t[...] = k_ref[...].astype(jnp.float32).T.astype(jnp.bfloat16)
        seg_row = seg_ref[...].astype(jnp.float32)
        seg_col = jnp.broadcast_to(seg_row, (BLOCK, window)).T
        row = lax.broadcasted_iota(jnp.int32, (window, BLOCK), 0)
        col = lax.broadcasted_iota(jnp.int32, (window, BLOCK), 1)
        for start in range(0, window, BLOCK):
            same = seg_col == seg_row[:, start:start + BLOCK]
            bias[:, start:start + BLOCK] = jnp.where(same & (row <= col + start), 0.0, MASKED)
        dk_acc[...] = jnp.zeros_like(dk_acc)
        dv_acc[...] = jnp.zeros_like(dv_acc)

    lse = lse_f[pl.ds(head, 1), :]
    delta = delta_f[pl.ds(head, 1), :]
    parts = []
    for start in range(0, window, BLOCK):
        rows = slice(start, start + BLOCK)
        query = q_ref[start:, :]
        dout = do_ref[start:, :]
        scores = nt(k_ref[rows, :], query)
        probs = jnp.exp2(scores * (scale * LOG2E) - lse[:, start:] + bias[rows, start:])
        grad_prob = nt(v_ref[rows, :], dout)
        grad_score = (probs * (grad_prob - delta[:, start:])).astype(jnp.bfloat16)
        dv_acc[rows, :] += nn(probs.astype(jnp.bfloat16), dout)
        dk_acc[rows, :] += nn(grad_score, query)
        parts.append(nn(key_t[:, rows], grad_score))
    for start in range(0, window, BLOCK):
        total = parts[0][:, start:start + BLOCK]
        for index in range(1, start // BLOCK + 1):
            first = start - index * BLOCK
            total += parts[index][:, first:first + BLOCK]
        out_ref[start:start + BLOCK, pl.ds(pl.multiple_of(head * size, size), size)] = (
            (total * scale).T.astype(jnp.bfloat16)
        )

    @pl.when(head == heads - 1)
    def _():
        out_ref[:, heads * size:(heads + 1) * size] = (dk_acc[...] * scale).astype(jnp.bfloat16)
        out_ref[:, (heads + 1) * size:] = dv_acc[...].astype(jnp.bfloat16)


def joined_gradients(query, dout, key, value, lse, delta, seg):
    window, width = query.shape
    size = key.shape[1]
    heads = width // size
    whole = lambda shape: pl.BlockSpec(shape, lambda r: (0, 0))
    per_head = pl.BlockSpec((window, size), lambda r: (0, r))
    return pl.pallas_call(
        attention_kernel,
        grid=(heads,),
        in_specs=[per_head, per_head, whole((window, size)), whole((window, size)),
                  whole((heads, window)), whole((heads, window)), whole((1, window))],
        out_specs=whole((window, width + 2 * size)),
        out_shape=jax.ShapeDtypeStruct((window, width + 2 * size), jnp.bfloat16),
        scratch_shapes=[
            pltpu.VMEM((window, window), jnp.float32),
            pltpu.VMEM((size, window), jnp.bfloat16),
            pltpu.VMEM((heads, window), jnp.float32),
            pltpu.VMEM((heads, window), jnp.float32),
            pltpu.VMEM((window, size), jnp.float32),
            pltpu.VMEM((window, size), jnp.float32),
        ],
        compiler_params=pltpu.CompilerParams(vmem_limit_bytes=24 << 20),
        cost_estimate=pl.CostEstimate(flops=4 * 10 ** 9, bytes_accessed=4 * 10 ** 6, transcendentals=10 ** 6),
        name="attention_backward",
    )(query, dout, key, value, lse, delta, seg)


def projection_kernel(where_ref, j0, jp, jm, jf, a_own, a1, a2, a3, a4, ax1, ax2, ax3, ax4,
                      b_own, b1, b2, bx1, bx2, out_ref, joined, wa, wb, sems):
    y, z, c, x = (where_ref[i] for i in range(4))
    sign = 1 - 2 * c
    count = [0]
    copies = []

    def copy(source, target):
        made = pltpu.make_async_copy(source, target, sems.at[count[0]])
        count[0] += 1
        made.start()
        copies.append(made)

    for source, step in ((j0, 0), (jp, 3), (jm, 1), (jf, 2)):
        copy(source, joined.at[(x + step) % 4])

    def put(buffer, source, g, slot):
        copy(source, buffer.at[g, pl.ds(pl.multiple_of(slot * BLOCK, BLOCK), BLOCK)])

    half_mine, half_theirs = c * 2, (1 - c) * 2
    for j in range(4):
        g = (y + j) % 4
        put(wa, a_own.at[j], g, z)
        for k, (mine, theirs) in enumerate(((a1, ax1), (a2, ax2), (a3, ax3)), 1):
            put(wa, mine.at[j], g, (z + 8 - sign * k) % 8)
            put(wa, theirs.at[j], g, (z + 8 + sign * k) % 8)
    for j in range(2):
        put(wa, a4.at[j], (y + half_mine + j) % 4, (z + 4) % 8)
        put(wa, ax4.at[j], (y + half_theirs + j) % 4, (z + 4) % 8)
    for k in range(8):
        step = (0, -1, -2, -3, 4, 1, 2, 3)[k]
        put(wb, b_own.at[k], y, (z + 8 + sign * step) % 8)
        put(wb, b1.at[k], (y + 4 - sign) % 4, (z + 8 + sign * step) % 8)
        put(wb, bx1.at[k], (y + 4 + sign) % 4, (z + 8 - sign * step) % 8)
    for k in range(4):
        mine = jnp.where(c == 0, (0, 7, 6, 5)[k], (1, 2, 3, 4)[k])
        theirs = jnp.where(c == 0, (1, 2, 3, 4)[k], (0, 7, 6, 5)[k])
        put(wb, b2.at[k], (y + 2) % 4, (z + mine) % 8)
        put(wb, bx2.at[k], (y + 2) % 4, (z + theirs) % 8)
    for made in copies:
        made.wait()
    half = wa.shape[2]
    for start in range(0, out_ref.shape[1], 256):
        total = None
        for g in range(4):
            for buffer, columns in ((wa, slice(0, half)), (wb, slice(half, 2 * half))):
                term = nt(joined[g, :, columns], buffer[g, start:start + 256, :])
                total = term if total is None else total + term
        out_ref[:, start:start + 256] = total.astype(jnp.bfloat16)


def projection(where, *operands):
    window, width = operands[0].shape
    half = width // 2
    columns = 8 * BLOCK
    return pl.pallas_call(
        projection_kernel,
        in_specs=[pl.BlockSpec(memory_space=pltpu.SMEM)]
        + [pl.BlockSpec(memory_space=pl.ANY)] * len(operands),
        out_specs=pl.BlockSpec(memory_space=pltpu.VMEM),
        out_shape=jax.ShapeDtypeStruct((window, columns), jnp.bfloat16),
        scratch_shapes=[
            pltpu.VMEM((4, window, width), jnp.bfloat16),
            pltpu.VMEM((4, columns, half), jnp.bfloat16),
            pltpu.VMEM((4, columns, half), jnp.bfloat16),
            pltpu.SemaphoreType.DMA((72,)),
        ],
        compiler_params=pltpu.CompilerParams(vmem_limit_bytes=32 << 20),
        cost_estimate=pl.CostEstimate(flops=6 * 10 ** 9, bytes_accessed=20 * 10 ** 6, transcendentals=0),
        name="projection",
    )(where, *operands)


def gather_weights(weight, core):
    rows, width = weight.shape
    half = width // 2
    turned = move(weight, ("y", "x"), lambda y, x: dict(y=x, x=y))
    other = swap_cores(turned)
    low = jnp.where(core == 0, turned, other)
    high = jnp.where(core == 0, other, turned)
    block = jnp.concatenate([low, high], axis=0)
    a_block, b_block = block[:, :half], block[:, half:]
    a_block, b_block = lax.optimization_barrier((a_block, b_block))

    a_ahead = shift(a_block, "y", -1)
    a_behind = shift(a_block, "y", 1)
    a_far = shift(a_block, "y", 2)
    b1 = along(b_block, "z", 1)
    b4 = along(lax.dynamic_slice_in_dim(b_block, core * rows, rows, 0), "z", 4)

    a_own = jnp.stack([a_block, a_ahead, a_far, a_behind])
    a1 = along(a_own, "z", 1)

    b23 = along(jnp.stack([b1, b_block]), "z", 2)
    bx1, bx4, bx23 = swap_cores(b1), swap_cores(b4), swap_cores(b23)
    far = jnp.concatenate([jnp.where(core == 0, b4, bx4), jnp.where(core == 0, bx4, b4)], axis=0)
    b_own = jnp.stack([b_block, b1, b23[1], b23[0], far, bx1, bx23[1], bx23[0]])

    a2 = along(a1, "z", 1)
    b_next = along(b_own, "y", 1)
    a3 = along(a2, "z", 1)
    a4 = along(lax.dynamic_slice_in_dim(a3, core * 2, 2, 0), "z", 1)
    b_far = along(lax.dynamic_slice_in_dim(b_next, core, 4, 0), "y", 1)
    mine = (a1, a2, a3, a4)
    theirs = tuple(swap_cores(v) for v in mine)
    return (a_own,) + mine + theirs + (b_own, b_next, b_far, swap_cores(b_next), swap_cores(b_far))


def on_device(query_rows, key_rows, value_rows, output_gradient, row_logsumexp, row_delta_sums,
              segments, query_key_value_weight):
    window, _, width = query_rows.shape
    place = [lax.axis_index(a) for a in ("y", "z", "c", "x")]
    core = place[2]
    token_index = (place[0] * SIZES["z"] + place[1]) * SIZES["c"] + core
    weights = gather_weights(query_key_value_weight[:, 0], core)
    seg = lax.dynamic_slice_in_dim(segments, token_index * window, window).reshape(1, window)
    joined = joined_gradients(
        query_rows.reshape(window, width), output_gradient.reshape(window, width),
        key_rows[:, 0], value_rows[:, 0], row_logsumexp[0], row_delta_sums[0], seg)
    from_below = shift(joined, "x", 1)
    from_above = shift(joined, "x", -1)
    from_far = shift(joined, "x", 2)
    where = jnp.stack(place).astype(jnp.int32)
    return projection(where, joined, from_below, from_above, from_far, *weights)


def solution(mesh):
    grid = Mesh(mesh.devices.reshape(4, 8, 2, 4), ("y", "z", "c", "x"))
    tok = ("y", "z", "c")
    rows = P(tok, "x", None)
    placed = (rows, rows, rows, rows, P("x", None, tok), P("x", None, tok), P(), rows)
    return jax.shard_map(on_device, mesh=grid, in_specs=placed, out_specs=P(tok, "x"), check_vma=False)
```

```python
import jax
import jax.numpy as jnp
import numpy as np
from jax import lax
from jax.experimental import pallas as pl
from jax.experimental.pallas import tpu as pltpu
from jax.sharding import Mesh, PartitionSpec as P

SIZES = {"y": 4, "z": 8, "c": 2, "x": 4}
BLOCK = 128
MASKED = -1e30
ATTENTION_VMEM = 58 << 20
PROJECT_VMEM = 16 << 20
Y_FIRST = 512
LOG2E = 1.4426950408889634


def move(value, axes, target):
    axes = tuple(a for a in SIZES if a in axes)
    dims = [SIZES[a] for a in axes]
    pairs = []
    for source in range(int(np.prod(dims))):
        coords = dict(zip(axes, (int(v) for v in np.unravel_index(source, dims))))
        goal = target(**coords)
        goal = [goal[a] % SIZES[a] for a in axes]
        pairs.append((source, int(np.ravel_multi_index(goal, dims))))
    return lax.ppermute(value, axes, pairs)


def swap_cores(value):
    return move(value, ("c",), lambda c: dict(c=1 - c))


def along(value, axis, steps):
    sign = lambda c: steps if c == 0 else -steps
    return move(value, (axis, "c"), lambda c, **k: {axis: k[axis] + sign(c), "c": c})


def shift(value, axis, steps):
    return move(value, (axis,), lambda **k: {axis: k[axis] + steps})


def nt(a, b):
    return lax.dot_general(a, b, (((1,), (1,)), ((), ())), preferred_element_type=jnp.float32)


def nn(a, b):
    return jnp.dot(a, b, preferred_element_type=jnp.float32)


def attention_kernel(q_ref, do_ref, k_ref, v_ref, lse_ref, delta_ref, seg_ref, out_ref,
                     bias, key_t, lse_f, delta_f, dk_acc, dv_acc):
    head = pl.program_id(0)
    heads = pl.num_programs(0)
    window, size = k_ref.shape
    scale = size ** -0.5

    @pl.when(head == 0)
    def _():
        lse_f[...] = lse_ref[...].astype(jnp.float32) * LOG2E
        delta_f[...] = delta_ref[...].astype(jnp.float32)
        key_t[...] = k_ref[...].astype(jnp.float32).T.astype(jnp.bfloat16)
        seg_row = seg_ref[...].astype(jnp.float32)
        seg_col = jnp.broadcast_to(seg_row, (BLOCK, window)).T
        row = lax.broadcasted_iota(jnp.int32, (window, BLOCK), 0)
        col = lax.broadcasted_iota(jnp.int32, (window, BLOCK), 1)
        for start in range(0, window, BLOCK):
            same = seg_col == seg_row[:, start:start + BLOCK]
            bias[:, start:start + BLOCK] = jnp.where(same & (row <= col + start), 0.0, MASKED)
        dk_acc[...] = jnp.zeros_like(dk_acc)
        dv_acc[...] = jnp.zeros_like(dv_acc)

    lse = lse_f[pl.ds(head, 1), :]
    delta = delta_f[pl.ds(head, 1), :]
    parts = []
    for start in range(0, window, BLOCK):
        rows = slice(start, start + BLOCK)
        query = q_ref[start:, :]
        dout = do_ref[start:, :]
        scores = nt(k_ref[rows, :], query)
        probs = jnp.exp2(scores * (scale * LOG2E) - lse[:, start:] + bias[rows, start:])
        grad_prob = nt(v_ref[rows, :], dout)
        grad_score = (probs * (grad_prob - delta[:, start:])).astype(jnp.bfloat16)
        dv_acc[rows, :] += nn(probs.astype(jnp.bfloat16), dout)
        dk_acc[rows, :] += nn(grad_score, query)
        parts.append(nn(key_t[:, rows], grad_score))
    for start in range(0, window, BLOCK):
        total = parts[0][:, start:start + BLOCK]
        for index in range(1, start // BLOCK + 1):
            first = start - index * BLOCK
            total += parts[index][:, first:first + BLOCK]
        out_ref[start:start + BLOCK, pl.ds(pl.multiple_of(head * size, size), size)] = (
            (total * scale).T.astype(jnp.bfloat16)
        )

    @pl.when(head == heads - 1)
    def _():
        out_ref[:, heads * size:(heads + 1) * size] = (dk_acc[...] * scale).astype(jnp.bfloat16)
        out_ref[:, (heads + 1) * size:] = dv_acc[...].astype(jnp.bfloat16)


def joined_gradients(query, dout, key, value, lse, delta, seg):
    window, width = query.shape
    size = key.shape[1]
    heads = width // size
    whole = lambda shape: pl.BlockSpec(shape, lambda r: (0, 0))
    per_head = pl.BlockSpec((window, size), lambda r: (0, r))
    return pl.pallas_call(
        attention_kernel,
        grid=(heads,),
        in_specs=[per_head, per_head, whole((window, size)), whole((window, size)),
                  whole((heads, window)), whole((heads, window)), whole((1, window))],
        out_specs=whole((window, width + 2 * size)),
        out_shape=jax.ShapeDtypeStruct((window, width + 2 * size), jnp.bfloat16),
        scratch_shapes=[
            pltpu.VMEM((window, window), jnp.float32),
            pltpu.VMEM((size, window), jnp.bfloat16),
            pltpu.VMEM((heads, window), jnp.float32),
            pltpu.VMEM((heads, window), jnp.float32),
            pltpu.VMEM((window, size), jnp.float32),
            pltpu.VMEM((window, size), jnp.float32),
        ],
        compiler_params=pltpu.CompilerParams(vmem_limit_bytes=ATTENTION_VMEM),
        cost_estimate=pl.CostEstimate(flops=4 * 10 ** 9, bytes_accessed=4 * 10 ** 6, transcendentals=10 ** 6),
        name="attention_backward",
    )(query, dout, key, value, lse, delta, seg)


def slot_offsets(c, part):
    sign = 1 - 2 * c
    first = 4 * c if part == "lo" else 4 - 4 * c
    step = -sign if part == "lo" else sign
    return [first] + [step * k for k in (1, 2, 3)]


class Plan:
    def __init__(self, joined, slots, rows, first, last):
        self.joined, self.slots, self.rows, self.first, self.last = joined, slots, rows, first, last


def projection_kernel(plan, where_ref, *refs):
    y, z, c, x = (where_ref[i] for i in range(4))
    sign = 1 - 2 * c
    refs = list(refs)
    acc_in = None if plan.first else refs.pop(0)
    heads = [refs.pop(0) for _ in plan.joined]
    slots = []
    for offset in plan.slots:
        slots.append([refs.pop(0), refs.pop(0)] if offset == "far" else [refs.pop(0)])
    rows = [refs.pop(0) for _ in plan.rows]
    out_ref, joined, acc = refs
    width = heads[0].shape[1]
    split = Y_FIRST

    def steps(offset):
        return 2 if offset in (2, "far") else sign * offset

    def tile(offset):
        return pl.ds(pl.multiple_of(((z + 8 + offset) % 8) * BLOCK, BLOCK), BLOCK)

    if plan.first:
        acc[...] = jnp.zeros_like(acc)
    else:
        acc[...] = acc_in[...]
    if plan.rows:
        for index, source in enumerate(heads):
            joined[index] = source[:, split:]

    def slot(sources, offset, g):
        if len(sources) == 2:
            k = (y - g + 4) % 4
            mine, theirs = sources
            from_zero = k < 2
            index_zero = jnp.where(from_zero, k, 0)
            index_one = jnp.where(from_zero, 0, (4 - k) % 4 - 1)
            index = jnp.where(from_zero, index_zero, index_one)
            holder = jnp.where(from_zero, 0, 1)
            return jnp.where(holder == c, mine[index], theirs[index])
        made_here = offset <= 0
        direction = sign if made_here else -sign
        return sources[0][((y - g) * direction + 4) % 4]

    for pair in range(0, len(slots), 2):
        total = None
        for source, head in zip(heads, plan.joined):
            g = (x + steps(head) + 4) % 4
            block = jnp.concatenate([slot(slots[pair + k], plan.slots[pair + k], g) for k in range(2)], axis=0)
            term = nt(source[:, :split], block)
            total = term if total is None else total + term
        for k in range(2):
            offset = plan.slots[pair + k]
            acc[:, tile(4 if offset == "far" else sign * offset)] += total[:, k * BLOCK:(k + 1) * BLOCK]

    for source, (part, same, offset, against) in zip(rows, plan.rows):
        g = (y + 4 + steps(offset)) % 4
        index = jnp.int32(-1)
        for position, head in enumerate(plan.joined):
            if head in against:
                index = jnp.where((x + steps(head) + 4) % 4 == g, position, index)
        offsets = slot_offsets(c if same else 1 - c, part)

        def body(source=source, index=index, offsets=offsets):
            for pair in (0, 2):
                block = source[pair:pair + 2].reshape(2 * BLOCK, width - split)
                term = nt(joined[index], block)
                for k in range(2):
                    acc[:, tile(offsets[pair + k])] += term[:, k * BLOCK:(k + 1) * BLOCK]

        if len(against) == 4:
            body()
        else:
            pl.when(index >= 0)(body)
    out_ref[...] = acc[...].astype(out_ref.dtype)


def projection(plan, name, where, *operands):
    window, width = operands[0 if plan.first else 1].shape
    columns = 8 * BLOCK
    vmem = pl.BlockSpec(memory_space=pltpu.VMEM)
    share = (len(plan.joined) * len(plan.slots) + len(plan.rows)) / 40
    return pl.pallas_call(
        lambda *refs: projection_kernel(plan, *refs),
        in_specs=[pl.BlockSpec(memory_space=pltpu.SMEM)] + [vmem] * len(operands),
        out_specs=vmem,
        out_shape=jax.ShapeDtypeStruct((window, columns), jnp.bfloat16 if plan.last else jnp.float32),
        scratch_shapes=[
            pltpu.VMEM((len(plan.joined) if plan.rows else 1, window, width - Y_FIRST), jnp.bfloat16),
            pltpu.VMEM((window, columns), jnp.float32),
        ],
        compiler_params=pltpu.CompilerParams(vmem_limit_bytes=PROJECT_VMEM),
        cost_estimate=pl.CostEstimate(
            flops=int(1e9 * share), bytes_accessed=int(1e6 * share), transcendentals=0),
        name=name,
    )(where, *operands)


ALL = (0, -1, 1, 2)
NEAR = (0, -1, 1)


def rows_of(against):
    return [("lo", True, 0, against), ("hi", True, 0, against), ("lo", True, -1, against),
            ("hi", True, -1, against), ("lo", False, 1, against), ("hi", False, 1, against)]


def in_order(*values):
    return lax.optimization_barrier(values)


def on_device(query_rows, key_rows, value_rows, output_gradient, row_logsumexp, row_delta_sums,
              segments, query_key_value_weight):
    window, _, width = query_rows.shape
    place = [lax.axis_index(a) for a in ("y", "z", "c", "x")]
    core = place[2]
    where = jnp.stack(place).astype(jnp.int32)
    token_index = (place[0] * SIZES["z"] + place[1]) * SIZES["c"] + core

    weight = query_key_value_weight[:, 0]
    rows = weight.shape[0]
    turned = move(weight, ("y", "x"), lambda y, x: dict(y=x, x=y))

    seg = lax.dynamic_slice_in_dim(segments, token_index * window, window).reshape(1, window)
    joined = joined_gradients(
        query_rows.reshape(window, width), output_gradient.reshape(window, width),
        key_rows[:, 0], value_rows[:, 0], row_logsumexp[0], row_delta_sums[0], seg)
    j_first = along(joined, "x", 1)

    turned, joined, where = in_order(turned, joined, where)
    other = swap_cores(turned)
    j_second = along(joined, "x", -1)
    block = jnp.concatenate([jnp.where(core == 0, turned, other), jnp.where(core == 0, other, turned)], axis=0)
    a_block, b_block = in_order(block[:, :Y_FIRST], block[:, Y_FIRST:])
    own_half = lax.dynamic_slice_in_dim(b_block, core * rows, rows, 0)

    b1 = along(b_block, "z", 1)
    a_first = along(a_block, "y", 1)
    a_second = along(a_block, "y", -1)
    a_far = along(a_block, "y", 2)
    b4 = along(own_half, "z", 4)
    b23 = along(jnp.stack([b1, b_block]), "z", 2)
    a_own = jnp.stack([a_block, a_first, a_far, a_second])
    a1 = along(a_own, "z", 1)
    x1, x4, x23 = swap_cores(b1), swap_cores(b4), swap_cores(b23)
    far = jnp.concatenate([jnp.where(core == 0, b4, x4), jnp.where(core == 0, x4, b4)], axis=0)
    lo = jnp.stack([jnp.where(core == 0, b_block, far), b1, b23[1], b23[0]])
    hi = jnp.stack([jnp.where(core == 0, far, b_block), x1, x23[1], x23[0]])
    lo, hi = in_order(lo, hi)
    lo_next = along(lo, "y", 1)
    a2 = along(a1, "z", 1)
    ax1 = swap_cores(a1)
    hi_next = along(hi, "y", 1)
    lo_far = along(lo_next, "y", 1)
    a3 = along(a2, "z", 1)
    ax2 = swap_cores(a2)
    lo_x, hi_x = swap_cores(lo_next), swap_cores(hi_next)
    j_far = along(j_first, "x", 1)
    a4 = along(lax.dynamic_slice_in_dim(a3, core, 2, 0), "z", 1)
    far_x = swap_cores(lo_far)
    ax3 = swap_cores(a3)
    ax4 = swap_cores(a4)

    ring = (a_own, a1, ax1, a2)
    near_rows = (lo, hi, lo_next, hi_next, lo_x, hi_x)
    acc = projection(Plan(NEAR, (0, -1, 1, -2), rows_of(NEAR), True, False), "project_near", where,
                     joined, j_first, j_second, *ring, *near_rows)
    acc = projection(Plan((2,), (0, -1, 1, -2), rows_of((2,)), False, False), "project_far_head", where,
                     acc, j_far, *ring, *near_rows)
    far_rows = [("lo", True, "far", ALL), ("lo", False, "far", ALL)]
    return projection(Plan(ALL, (2, -3, 3, "far"), far_rows, False, True), "project_rest", where,
                      acc, joined, j_first, j_second, j_far, ax2, a3, ax3, a4, ax4, lo_far, far_x)


def solution(mesh):
    grid = Mesh(mesh.devices.reshape(4, 8, 2, 4), ("y", "z", "c", "x"))
    tok = ("y", "z", "c")
    rows = P(tok, "x", None)
    placed = (rows, rows, rows, rows, P("x", None, tok), P("x", None, tok), P(), rows)
    return jax.shard_map(on_device, mesh=grid, in_specs=placed, out_specs=P(tok, "x"), check_vma=False)
```

```python
import jax
import jax.numpy as jnp
import numpy as np
from jax import lax
from jax.experimental import pallas as pl
from jax.experimental.pallas import tpu as pltpu
from jax.sharding import Mesh, PartitionSpec as P

SIZES = {"y": 4, "z": 8, "c": 2, "x": 4}
BLOCK = 128
MASKED = -1e30
ATTENTION_VMEM = 58 << 20
STRIP = 256
PROJECT_VMEM = 16 << 20
Y_FIRST = 512
LOG2E = 1.4426950408889634


def move(value, axes, target):
    axes = tuple(a for a in SIZES if a in axes)
    dims = [SIZES[a] for a in axes]
    pairs = []
    for source in range(int(np.prod(dims))):
        coords = dict(zip(axes, (int(v) for v in np.unravel_index(source, dims))))
        goal = target(**coords)
        goal = [goal[a] % SIZES[a] for a in axes]
        pairs.append((source, int(np.ravel_multi_index(goal, dims))))
    return lax.ppermute(value, axes, pairs)


def swap_cores(value):
    return move(value, ("c",), lambda c: dict(c=1 - c))


def along(value, axis, steps):
    sign = lambda c: steps if c == 0 else -steps
    return move(value, (axis, "c"), lambda c, **k: {axis: k[axis] + sign(c), "c": c})


def shift(value, axis, steps):
    return move(value, (axis,), lambda **k: {axis: k[axis] + steps})


def nt(a, b):
    return lax.dot_general(a, b, (((1,), (1,)), ((), ())), preferred_element_type=jnp.float32)


def nn(a, b):
    return jnp.dot(a, b, preferred_element_type=jnp.float32)


def attention_kernel(q_hbm, do_hbm, k_hbm, v_hbm, lse_hbm, delta_hbm, seg_ref, out_ref,
                     query_all, dout_all, k_ref, v_ref, lse_b, delta_b, bias, key_t, dk_acc, dv_acc, sems):
    heads, window, size = query_all.shape
    scale = size ** -0.5
    small = [pltpu.make_async_copy(source, target, sems.at[2 * heads + index]) for index, (source, target) in
             enumerate(((k_hbm, k_ref), (v_hbm, v_ref), (lse_hbm, lse_b), (delta_hbm, delta_b)))]
    for made in small:
        made.start()
    wide = []
    for head in range(heads):
        columns = slice(head * size, (head + 1) * size)
        wide.append([
            pltpu.make_async_copy(q_hbm.at[:, columns], query_all.at[head], sems.at[2 * head]),
            pltpu.make_async_copy(do_hbm.at[:, columns], dout_all.at[head], sems.at[2 * head + 1])])
        for made in wide[-1]:
            made.start()
    seg_row = seg_ref[...].astype(jnp.float32)
    seg_col = jnp.broadcast_to(seg_row, (BLOCK, window)).T
    row = lax.broadcasted_iota(jnp.int32, (window, BLOCK), 0)
    col = lax.broadcasted_iota(jnp.int32, (window, BLOCK), 1)
    for start in range(0, window, BLOCK):
        same = seg_col == seg_row[:, start:start + BLOCK]
        bias[:, start:start + BLOCK] = jnp.where(same & (row <= col + start), 0.0, MASKED)
    for made in small:
        made.wait()
    lse_f = lse_b[...].astype(jnp.float32) * LOG2E
    delta_f = delta_b[...].astype(jnp.float32)
    key_t[...] = k_ref[...].astype(jnp.float32).T.astype(jnp.bfloat16)
    for head in range(heads):
        for made in wide[head]:
            made.wait()
        lse = lse_f[head:head + 1, :]
        delta = delta_f[head:head + 1, :]
        for start in range(0, window, STRIP):
            rows = slice(start, start + STRIP)
            query = query_all[head, start:, :]
            dout = dout_all[head, start:, :]
            scores = nt(k_ref[rows, :], query)
            probs = jnp.exp2(scores * (scale * LOG2E) - lse[:, start:] + bias[rows, start:])
            grad_prob = nt(v_ref[rows, :], dout)
            grad_score = (probs * (grad_prob - delta[:, start:])).astype(jnp.bfloat16)
            dv = nn(probs.astype(jnp.bfloat16), dout)
            dk = nn(grad_score, query)
            part = nn(key_t[:, rows], grad_score)
            if head == 0:
                dv_acc[rows, :] = dv
                dk_acc[rows, :] = dk
            else:
                dv_acc[rows, :] += dv
                dk_acc[rows, :] += dk
            if start == 0:
                total = part
            else:
                total = jnp.concatenate([total[:, :start], total[:, start:] + part], axis=1)
        out_ref[:, head * size:(head + 1) * size] = (total * scale).T.astype(jnp.bfloat16)
    out_ref[:, heads * size:(heads + 1) * size] = (dk_acc[...] * scale).astype(jnp.bfloat16)
    out_ref[:, (heads + 1) * size:] = dv_acc[...].astype(jnp.bfloat16)


def joined_gradients(query, dout, key, value, lse, delta, seg):
    window, width = query.shape
    size = key.shape[1]
    heads = width // size
    hbm = pl.BlockSpec(memory_space=pltpu.HBM)
    vmem = pl.BlockSpec(memory_space=pltpu.VMEM)
    return pl.pallas_call(
        attention_kernel,
        in_specs=[hbm] * 6 + [vmem],
        out_specs=vmem,
        out_shape=jax.ShapeDtypeStruct((window, width + 2 * size), jnp.bfloat16),
        scratch_shapes=[
            pltpu.VMEM((heads, window, size), jnp.bfloat16),
            pltpu.VMEM((heads, window, size), jnp.bfloat16),
            pltpu.VMEM((window, size), jnp.bfloat16),
            pltpu.VMEM((window, size), jnp.bfloat16),
            pltpu.VMEM((heads, window), jnp.bfloat16),
            pltpu.VMEM((heads, window), jnp.bfloat16),
            pltpu.VMEM((window, window), jnp.float32),
            pltpu.VMEM((size, window), jnp.bfloat16),
            pltpu.VMEM((window, size), jnp.float32),
            pltpu.VMEM((window, size), jnp.float32),
            pltpu.SemaphoreType.DMA((2 * heads + 4,)),
        ],
        compiler_params=pltpu.CompilerParams(vmem_limit_bytes=ATTENTION_VMEM),
        cost_estimate=pl.CostEstimate(flops=4 * 10 ** 9, bytes_accessed=4 * 10 ** 6, transcendentals=10 ** 6),
        name="attention_backward",
    )(query, dout, key, value, lse, delta, seg)


def slot_offsets(c, part):
    sign = 1 - 2 * c
    first = 4 * c if part == "lo" else 4 - 4 * c
    step = -sign if part == "lo" else sign
    return [first] + [step * k for k in (1, 2, 3)]


class Plan:
    def __init__(self, joined, slots, rows, first, last):
        self.joined, self.slots, self.rows, self.first, self.last = joined, slots, rows, first, last


def projection_kernel(plan, where_ref, *refs):
    y, z, c, x = (where_ref[i] for i in range(4))
    sign = 1 - 2 * c
    refs = list(refs)
    acc_in = None if plan.first else refs.pop(0)
    heads = [refs.pop(0) for _ in plan.joined]
    slots = []
    for offset in plan.slots:
        slots.append([refs.pop(0), refs.pop(0)] if offset == "far" else [refs.pop(0)])
    rows = [refs.pop(0) for _ in plan.rows]
    out_ref, joined = refs[:2]
    acc = refs[2] if plan.last else out_ref
    width = heads[0].shape[1]
    split = Y_FIRST

    def steps(offset):
        return 2 if offset in (2, "far") else sign * offset

    def tile(offset):
        return pl.ds(pl.multiple_of(((z + 8 + offset) % 8) * BLOCK, BLOCK), BLOCK)

    if plan.first:
        acc[...] = jnp.zeros_like(acc)
    else:
        acc[...] = acc_in[...]
    for position, (source, head) in enumerate(zip(heads, plan.joined)):
        if len(plan.rows) == 2:
            g = (y + 4 + steps(plan.rows[0][2])) % 4

            @pl.when((x + steps(head) + 4) % 4 == g)
            def _(source=source):
                joined[0] = source[:, split:]
        else:
            joined[position] = source[:, split:]

    def slot(sources, offset, g):
        if len(sources) == 2:
            k = (y - g + 4) % 4
            mine, theirs = sources
            from_zero = k < 2
            index_zero = jnp.where(from_zero, k, 0)
            index_one = jnp.where(from_zero, 0, (4 - k) % 4 - 1)
            index = jnp.where(from_zero, index_zero, index_one)
            holder = jnp.where(from_zero, 0, 1)
            return jnp.where(holder == c, mine[index], theirs[index])
        made_here = offset <= 0
        direction = sign if made_here else -sign
        return sources[0][((y - g) * direction + 4) % 4]

    for pair in range(0, len(slots), 2):
        total = None
        for source, head in zip(heads, plan.joined):
            g = (x + steps(head) + 4) % 4
            block = jnp.concatenate([slot(slots[pair + k], plan.slots[pair + k], g) for k in range(2)], axis=0)
            term = nt(source[:, :split], block)
            total = term if total is None else total + term
        for k in range(2):
            offset = plan.slots[pair + k]
            acc[:, tile(4 if offset == "far" else sign * offset)] += total[:, k * BLOCK:(k + 1) * BLOCK]

    for source, (part, same, offset, against) in zip(rows, plan.rows):
        g = (y + 4 + steps(offset)) % 4
        index = jnp.int32(-1)
        for position, head in enumerate(plan.joined):
            if head in against:
                index = jnp.where((x + steps(head) + 4) % 4 == g, 0 if len(plan.rows) == 2 else position, index)
        offsets = slot_offsets(c if same else 1 - c, part)

        def body(source=source, index=index, offsets=offsets):
            for pair in (0, 2):
                block = source[pair:pair + 2].reshape(2 * BLOCK, width - split)
                term = nt(joined[index], block)
                for k in range(2):
                    acc[:, tile(offsets[pair + k])] += term[:, k * BLOCK:(k + 1) * BLOCK]

        if len(against) == 4:
            body()
        else:
            pl.when(index >= 0)(body)
    if plan.last:
        out_ref[...] = acc[...].astype(out_ref.dtype)


def projection(plan, name, where, *operands):
    window, width = operands[0 if plan.first else 1].shape
    columns = 8 * BLOCK
    vmem = pl.BlockSpec(memory_space=pltpu.VMEM)
    share = (len(plan.joined) * len(plan.slots) + len(plan.rows)) / 40
    return pl.pallas_call(
        lambda *refs: projection_kernel(plan, *refs),
        in_specs=[pl.BlockSpec(memory_space=pltpu.SMEM)] + [vmem] * len(operands),
        out_specs=vmem,
        out_shape=jax.ShapeDtypeStruct((window, columns), jnp.bfloat16 if plan.last else jnp.float32),
        scratch_shapes=[
            pltpu.VMEM((1 if len(plan.rows) == 2 else len(plan.joined), window, width - Y_FIRST), jnp.bfloat16),
        ] + [pltpu.VMEM((window, columns), jnp.float32)] * plan.last,
        compiler_params=pltpu.CompilerParams(vmem_limit_bytes=PROJECT_VMEM),
        cost_estimate=pl.CostEstimate(
            flops=int(1e9 * share), bytes_accessed=int(1e6 * share), transcendentals=0),
        name=name,
    )(where, *operands)


ALL = (0, -1, 1, 2)
NEAR = (0, -1, 1)


def rows_of(against):
    return [("lo", True, 0, against), ("hi", True, 0, against), ("lo", True, -1, against),
            ("hi", True, -1, against), ("lo", False, 1, against), ("hi", False, 1, against)]


def in_order(*values):
    return lax.optimization_barrier(values)


def on_device(query_rows, key_rows, value_rows, output_gradient, row_logsumexp, row_delta_sums,
              segments, query_key_value_weight):
    window, _, width = query_rows.shape
    place = [lax.axis_index(a) for a in ("y", "z", "c", "x")]
    core = place[2]
    where = jnp.stack(place).astype(jnp.int32)
    token_index = (place[0] * SIZES["z"] + place[1]) * SIZES["c"] + core

    weight = query_key_value_weight[:, 0]
    rows = weight.shape[0]
    turned = move(weight, ("y", "x"), lambda y, x: dict(y=x, x=y))

    seg = lax.dynamic_slice_in_dim(segments, token_index * window, window).reshape(1, window)
    joined = joined_gradients(
        query_rows.reshape(window, width), output_gradient.reshape(window, width),
        key_rows[:, 0], value_rows[:, 0], row_logsumexp[0], row_delta_sums[0], seg)
    j_first = along(joined, "x", 1)

    turned, joined, where = in_order(turned, joined, where)
    other = swap_cores(turned)
    j_second = along(joined, "x", -1)
    block = jnp.concatenate([jnp.where(core == 0, turned, other), jnp.where(core == 0, other, turned)], axis=0)
    a_block, b_block = in_order(block[:, :Y_FIRST], block[:, Y_FIRST:])
    own_half = lax.dynamic_slice_in_dim(b_block, core * rows, rows, 0)

    b1 = along(b_block, "z", 1)
    a_first = along(a_block, "y", 1)
    a_second = along(a_block, "y", -1)
    a_far = along(a_block, "y", 2)
    b4 = along(own_half, "z", 4)
    b23 = along(jnp.stack([b1, b_block]), "z", 2)
    a_own = jnp.stack([a_block, a_first, a_far, a_second])
    a1 = along(a_own, "z", 1)
    x1, x4, x23 = swap_cores(b1), swap_cores(b4), swap_cores(b23)
    far = jnp.concatenate([jnp.where(core == 0, b4, x4), jnp.where(core == 0, x4, b4)], axis=0)
    lo = jnp.stack([jnp.where(core == 0, b_block, far), b1, b23[1], b23[0]])
    hi = jnp.stack([jnp.where(core == 0, far, b_block), x1, x23[1], x23[0]])
    lo, hi = in_order(lo, hi)
    lo_next = along(lo, "y", 1)
    a2 = along(a1, "z", 1)
    ax1 = swap_cores(a1)
    hi_next = along(hi, "y", 1)
    lo_far = along(lo_next, "y", 1)
    a3 = along(a2, "z", 1)
    ax2 = swap_cores(a2)
    lo_x, hi_x = swap_cores(lo_next), swap_cores(hi_next)
    j_far = along(j_first, "x", 1)
    a4 = along(lax.dynamic_slice_in_dim(a3, core, 2, 0), "z", 1)

    ring = (a_own, a1, ax1, a2)
    near_rows = (lo, hi, lo_next, hi_next, lo_x, hi_x)
    acc = projection(Plan(NEAR, (0, -1, 1, -2), rows_of(NEAR), True, False), "project_near", where,
                     joined, j_first, j_second, *ring, *near_rows)
    acc, lo_far, a4 = in_order(acc, lo_far, a4)
    far_x = swap_cores(lo_far)
    ax3 = swap_cores(a3)
    ax4 = swap_cores(a4)
    acc = projection(Plan((2,), (0, -1, 1, -2), rows_of((2,)), False, False), "project_far_head", where,
                     acc, j_far, *ring, *near_rows)
    far_rows = [("lo", True, "far", ALL), ("lo", False, "far", ALL)]
    return projection(Plan(ALL, (2, -3, 3, "far"), far_rows, False, True), "project_rest", where,
                      acc, joined, j_first, j_second, j_far, ax2, a3, ax3, a4, ax4, lo_far, far_x)


def solution(mesh):
    grid = Mesh(mesh.devices.reshape(4, 8, 2, 4), ("y", "z", "c", "x"))
    tok = ("y", "z", "c")
    rows = P(tok, "x", None)
    placed = (rows, rows, rows, rows, P("x", None, tok), P("x", None, tok), P(), rows)
    return jax.shard_map(on_device, mesh=grid, in_specs=placed, out_specs=P(tok, "x"), check_vma=False)
```

```python
import jax
import jax.numpy as jnp
import numpy as np
from jax import lax
from jax.experimental import pallas as pl
from jax.experimental.pallas import tpu as pltpu
from jax.sharding import Mesh, PartitionSpec as P

SIZES = {"y": 4, "z": 8, "c": 2, "x": 4}
BLOCK = 128
MASKED = -1e30
ATTENTION_VMEM = 58 << 20
STRIP = 256
PROJECT_VMEM = 28 << 20
Y_FIRST = 512
LOG2E = 1.4426950408889634


def move(value, axes, target):
    axes = tuple(a for a in SIZES if a in axes)
    dims = [SIZES[a] for a in axes]
    pairs = []
    for source in range(int(np.prod(dims))):
        coords = dict(zip(axes, (int(v) for v in np.unravel_index(source, dims))))
        goal = target(**coords)
        goal = [goal[a] % SIZES[a] for a in axes]
        pairs.append((source, int(np.ravel_multi_index(goal, dims))))
    return lax.ppermute(value, axes, pairs)


def swap_cores(value):
    return move(value, ("c",), lambda c: dict(c=1 - c))


def along(value, axis, steps):
    sign = lambda c: steps if c == 0 else -steps
    return move(value, (axis, "c"), lambda c, **k: {axis: k[axis] + sign(c), "c": c})


def shift(value, axis, steps):
    return move(value, (axis,), lambda **k: {axis: k[axis] + steps})


def nt(a, b):
    return lax.dot_general(a, b, (((1,), (1,)), ((), ())), preferred_element_type=jnp.float32)


def nn(a, b):
    return jnp.dot(a, b, preferred_element_type=jnp.float32)


def attention_kernel(q_hbm, do_hbm, k_hbm, v_hbm, lse_hbm, delta_hbm, seg_ref, out_ref,
                     query_all, dout_all, k_ref, v_ref, lse_b, delta_b, bias, key_t, dk_acc, dv_acc, sems):
    heads, window, size = query_all.shape
    scale = size ** -0.5
    small = [pltpu.make_async_copy(source, target, sems.at[2 * heads + index]) for index, (source, target) in
             enumerate(((k_hbm, k_ref), (v_hbm, v_ref), (lse_hbm, lse_b), (delta_hbm, delta_b)))]
    for made in small:
        made.start()
    wide = []
    for head in range(heads):
        columns = slice(head * size, (head + 1) * size)
        wide.append([
            pltpu.make_async_copy(q_hbm.at[:, columns], query_all.at[head], sems.at[2 * head]),
            pltpu.make_async_copy(do_hbm.at[:, columns], dout_all.at[head], sems.at[2 * head + 1])])
        for made in wide[-1]:
            made.start()
    seg_row = seg_ref[...].astype(jnp.float32)
    seg_col = jnp.broadcast_to(seg_row, (BLOCK, window)).T
    row = lax.broadcasted_iota(jnp.int32, (window, BLOCK), 0)
    col = lax.broadcasted_iota(jnp.int32, (window, BLOCK), 1)
    for start in range(0, window, BLOCK):
        same = seg_col == seg_row[:, start:start + BLOCK]
        bias[:, start:start + BLOCK] = jnp.where(same & (row <= col + start), 0.0, MASKED)
    for made in small:
        made.wait()
    lse_f = lse_b[...].astype(jnp.float32) * LOG2E
    delta_f = delta_b[...].astype(jnp.float32)
    key_t[...] = k_ref[...].astype(jnp.float32).T.astype(jnp.bfloat16)
    for head in range(heads):
        for made in wide[head]:
            made.wait()
        lse = lse_f[head:head + 1, :]
        delta = delta_f[head:head + 1, :]
        for start in range(0, window, STRIP):
            rows = slice(start, start + STRIP)
            query = query_all[head, start:, :]
            dout = dout_all[head, start:, :]
            scores = nt(k_ref[rows, :], query)
            probs = jnp.exp2(scores * (scale * LOG2E) - lse[:, start:] + bias[rows, start:])
            grad_prob = nt(v_ref[rows, :], dout)
            grad_score = (probs * (grad_prob - delta[:, start:])).astype(jnp.bfloat16)
            dv = nn(probs.astype(jnp.bfloat16), dout)
            dk = nn(grad_score, query)
            part = nn(key_t[:, rows], grad_score)
            if head == 0:
                dv_acc[rows, :] = dv
                dk_acc[rows, :] = dk
            else:
                dv_acc[rows, :] += dv
                dk_acc[rows, :] += dk
            if start == 0:
                total = part
            else:
                total = jnp.concatenate([total[:, :start], total[:, start:] + part], axis=1)
        out_ref[:, head * size:(head + 1) * size] = (total * scale).T.astype(jnp.bfloat16)
    out_ref[:, heads * size:(heads + 1) * size] = (dk_acc[...] * scale).astype(jnp.bfloat16)
    out_ref[:, (heads + 1) * size:] = dv_acc[...].astype(jnp.bfloat16)


def joined_gradients(query, dout, key, value, lse, delta, seg):
    window, width = query.shape
    size = key.shape[1]
    heads = width // size
    hbm = pl.BlockSpec(memory_space=pltpu.HBM)
    vmem = pl.BlockSpec(memory_space=pltpu.VMEM)
    return pl.pallas_call(
        attention_kernel,
        in_specs=[hbm] * 6 + [vmem],
        out_specs=vmem,
        out_shape=jax.ShapeDtypeStruct((window, width + 2 * size), jnp.bfloat16),
        scratch_shapes=[
            pltpu.VMEM((heads, window, size), jnp.bfloat16),
            pltpu.VMEM((heads, window, size), jnp.bfloat16),
            pltpu.VMEM((window, size), jnp.bfloat16),
            pltpu.VMEM((window, size), jnp.bfloat16),
            pltpu.VMEM((heads, window), jnp.bfloat16),
            pltpu.VMEM((heads, window), jnp.bfloat16),
            pltpu.VMEM((window, window), jnp.float32),
            pltpu.VMEM((size, window), jnp.bfloat16),
            pltpu.VMEM((window, size), jnp.float32),
            pltpu.VMEM((window, size), jnp.float32),
            pltpu.SemaphoreType.DMA((2 * heads + 4,)),
        ],
        compiler_params=pltpu.CompilerParams(vmem_limit_bytes=ATTENTION_VMEM),
        cost_estimate=pl.CostEstimate(flops=4 * 10 ** 9, bytes_accessed=4 * 10 ** 6, transcendentals=10 ** 6),
        name="attention_backward",
    )(query, dout, key, value, lse, delta, seg)


def slot_offsets(c, part):
    sign = 1 - 2 * c
    first = 4 * c if part == "lo" else 4 - 4 * c
    step = -sign if part == "lo" else sign
    return [first] + [step * k for k in (1, 2, 3)]


class Plan:
    def __init__(self, joined, slots, rows, first, last):
        self.joined, self.slots, self.rows, self.first, self.last = joined, slots, rows, first, last


def projection_kernel(plan, where_ref, *refs):
    y, z, c, x = (where_ref[i] for i in range(4))
    sign = 1 - 2 * c
    refs = list(refs)
    acc_in = None if plan.first else refs.pop(0)
    heads = [refs.pop(0) for _ in plan.joined]
    slots = []
    for offset in plan.slots:
        slots.append([refs.pop(0), refs.pop(0)] if offset == "far" else [refs.pop(0)])
    rows = [refs.pop(0) for _ in plan.rows]
    out_ref, ja, jb, wa, far, wb, sems = refs[:7]
    acc = refs[7] if plan.last else out_ref
    split = Y_FIRST
    single = len(plan.joined) == 1
    one_row_head = len(plan.rows) == 2

    def steps(offset):
        return 2 if offset in (2, "far") else sign * offset

    def tile(offset):
        return (z + 8 + offset) % 8

    def head_index(head):
        return (x + steps(head) + 4) % 4

    used = [0]

    def copy(source, target):
        made = pltpu.make_async_copy(source, target, sems.at[used[0]])
        used[0] += 1
        return made

    def entry(offset, g):
        return ((y - g) * (sign if offset <= 0 else -sign) + 4) % 4

    ahead = [copy(source.at[:, :split], ja.at[index]) for index, source in enumerate(heads)]
    for index, (sources, offset) in enumerate(zip(slots, plan.slots)):
        if offset == "far":
            ahead += [copy(source, far.at[which]) for which, source in enumerate(sources)]
        elif single:
            ahead.append(copy(sources[0].at[entry(offset, head_index(plan.joined[0]))], wa.at[index, 0]))
        else:
            ahead.append(copy(sources[0], wa.at[index]))
    for made in ahead:
        made.start()

    meets = []
    for part, same, offset, against in plan.rows:
        g = (y + 4 + steps(offset)) % 4
        index = jnp.int32(-1)
        for position, head in enumerate(plan.joined):
            if head in against:
                index = jnp.where(head_index(head) == g, position, index)
        meets.append((g, index, len(against) == 4))

    def guarded(sure, index, body):
        body() if sure else pl.when(index >= 0)(body)

    row_heads = []
    if one_row_head:
        for position, source in enumerate(heads):
            made = pltpu.make_async_copy(source.at[:, split:], jb.at[0], sems.at[used[0]])
            pl.when(meets[0][1] == position)(made.start)
            row_heads.append(made)
        used[0] += 1
    else:
        row_heads = [copy(source.at[:, split:], jb.at[position]) for position, source in enumerate(heads)]
        for made in row_heads:
            made.start()
    row_copies = []
    for index, (source, (g, meet, sure)) in enumerate(zip(rows, meets)):
        made = copy(source, wb.at[index])
        guarded(sure, meet, made.start)
        row_copies.append(made)

    if plan.first:
        acc[...] = jnp.zeros_like(acc)
    else:
        acc[...] = acc_in[...]

    for made in ahead:
        made.wait()

    def slot(index, offset, g):
        if offset == "far":
            k = (y - g + 4) % 4
            from_zero = k < 2
            place = jnp.where(from_zero, k, (4 - k) % 4 - 1)
            return far[jnp.where(jnp.where(from_zero, 0, 1) == c, 0, 1), jnp.maximum(place, 0)]
        return wa[index, 0 if single else entry(offset, g)]

    for pair in range(0, len(slots), 2):
        total = None
        for position, head in enumerate(plan.joined):
            g = head_index(head)
            block = jnp.concatenate([slot(pair + k, plan.slots[pair + k], g) for k in range(2)], axis=0)
            term = nt(ja[position], block)
            total = term if total is None else total + term
        for k in range(2):
            offset = plan.slots[pair + k]
            acc[tile(4 if offset == "far" else sign * offset)] += total[:, k * BLOCK:(k + 1) * BLOCK]

    if one_row_head:
        row_heads[0].wait()
    else:
        for made in row_heads:
            made.wait()
    for index, ((part, same, offset, against), (g, meet, sure)) in enumerate(zip(plan.rows, meets)):
        offsets = slot_offsets(c if same else 1 - c, part)

        def body(index=index, meet=meet, offsets=offsets):
            row_copies[index].wait()
            left = jb[0] if one_row_head or single else jb[meet]
            for pair in (0, 2):
                term = nt(left, wb[index, pair:pair + 2].reshape(2 * BLOCK, wb.shape[3]))
                for k in range(2):
                    acc[tile(offsets[pair + k])] += term[:, k * BLOCK:(k + 1) * BLOCK]

        guarded(sure, meet, body)
    if plan.last:
        for place in range(8):
            out_ref[:, place * BLOCK:(place + 1) * BLOCK] = acc[place].astype(out_ref.dtype)


def projection(plan, name, where, *operands):
    window, width = operands[0 if plan.first else 1].shape
    columns = 8 * BLOCK
    vmem = pl.BlockSpec(memory_space=pltpu.VMEM)
    kept = 0 if plan.first else 1
    heads, slots, rows = len(plan.joined), len(plan.slots), len(plan.rows)
    share = (heads * slots + rows) / 40
    return pl.pallas_call(
        lambda *refs: projection_kernel(plan, *refs),
        in_specs=[pl.BlockSpec(memory_space=pltpu.SMEM)] + [vmem] * kept
        + [pl.BlockSpec(memory_space=pl.ANY)] * (len(operands) - kept),
        out_specs=vmem,
        out_shape=jax.ShapeDtypeStruct((window, columns), jnp.bfloat16) if plan.last
        else jax.ShapeDtypeStruct((8, window, BLOCK), jnp.float32),
        scratch_shapes=[
            pltpu.VMEM((heads, window, Y_FIRST), jnp.bfloat16),
            pltpu.VMEM((1 if rows == 2 else heads, window, width - Y_FIRST), jnp.bfloat16),
            pltpu.VMEM((slots, 1 if heads == 1 else 4, BLOCK, Y_FIRST), jnp.bfloat16),
            pltpu.VMEM((2, 2, BLOCK, Y_FIRST), jnp.bfloat16),
            pltpu.VMEM((rows, 4, BLOCK, width - Y_FIRST), jnp.bfloat16),
            pltpu.SemaphoreType.DMA((24,)),
        ] + [pltpu.VMEM((8, window, BLOCK), jnp.float32)] * plan.last,
        compiler_params=pltpu.CompilerParams(vmem_limit_bytes=PROJECT_VMEM),
        cost_estimate=pl.CostEstimate(
            flops=int(1e9 * share), bytes_accessed=int(1e6 * share), transcendentals=0),
        name=name,
    )(where, *operands)


ALL = (0, -1, 1, 2)
NEAR = (0, -1, 1)


def rows_of(against):
    return [("lo", True, 0, against), ("hi", True, 0, against), ("lo", True, -1, against),
            ("hi", True, -1, against), ("lo", False, 1, against), ("hi", False, 1, against)]


def in_order(*values):
    return lax.optimization_barrier(values)


def on_device(query_rows, key_rows, value_rows, output_gradient, row_logsumexp, row_delta_sums,
              segments, query_key_value_weight):
    window, _, width = query_rows.shape
    place = [lax.axis_index(a) for a in ("y", "z", "c", "x")]
    core = place[2]
    where = jnp.stack(place).astype(jnp.int32)
    token_index = (place[0] * SIZES["z"] + place[1]) * SIZES["c"] + core

    weight = query_key_value_weight[:, 0]
    rows = weight.shape[0]
    turned = move(weight, ("y", "x"), lambda y, x: dict(y=x, x=y))

    seg = lax.dynamic_slice_in_dim(segments, token_index * window, window).reshape(1, window)
    joined = joined_gradients(
        query_rows.reshape(window, width), output_gradient.reshape(window, width),
        key_rows[:, 0], value_rows[:, 0], row_logsumexp[0], row_delta_sums[0], seg)
    j_first = along(joined, "x", 1)

    turned, joined, where = in_order(turned, joined, where)
    other = swap_cores(turned)
    j_second = along(joined, "x", -1)
    block = jnp.concatenate([jnp.where(core == 0, turned, other), jnp.where(core == 0, other, turned)], axis=0)
    a_block, b_block = in_order(block[:, :Y_FIRST], block[:, Y_FIRST:])
    own_half = lax.dynamic_slice_in_dim(b_block, core * rows, rows, 0)

    b1 = along(b_block, "z", 1)
    a_first = along(a_block, "y", 1)
    a_second = along(a_block, "y", -1)
    a_far = along(a_block, "y", 2)
    b4 = along(own_half, "z", 4)
    b23 = along(jnp.stack([b1, b_block]), "z", 2)
    a_own = jnp.stack([a_block, a_first, a_far, a_second])
    a1 = along(a_own, "z", 1)
    x1, x4, x23 = swap_cores(b1), swap_cores(b4), swap_cores(b23)
    far = jnp.concatenate([jnp.where(core == 0, b4, x4), jnp.where(core == 0, x4, b4)], axis=0)
    lo = jnp.stack([jnp.where(core == 0, b_block, far), b1, b23[1], b23[0]])
    hi = jnp.stack([jnp.where(core == 0, far, b_block), x1, x23[1], x23[0]])
    lo, hi = in_order(lo, hi)
    lo_next = along(lo, "y", 1)
    a2 = along(a1, "z", 1)
    ax1 = swap_cores(a1)
    hi_next = along(hi, "y", 1)
    lo_far = along(lo_next, "y", 1)
    a3 = along(a2, "z", 1)
    ax2 = swap_cores(a2)
    lo_x, hi_x = swap_cores(lo_next), swap_cores(hi_next)
    j_far = along(j_first, "x", 1)
    a4 = along(jnp.where(core == 0, a3[:2], a3[1:3]), "z", 1)

    ring = (a_own, a1, ax1, a2)
    near_rows = (lo, hi, lo_next, hi_next, lo_x, hi_x)
    acc = projection(Plan(NEAR, (0, -1, 1, -2), rows_of(NEAR), True, False), "project_near", where,
                     joined, j_first, j_second, *ring, *near_rows)
    acc, lo_far, a4 = in_order(acc, lo_far, a4)
    far_x = swap_cores(lo_far)
    ax3 = swap_cores(a3)
    ax4 = swap_cores(a4)
    acc = projection(Plan((2,), (0, -1, 1, -2), rows_of((2,)), False, False), "project_far_head", where,
                     acc, j_far, *ring, *near_rows)
    far_rows = [("lo", True, "far", ALL), ("lo", False, "far", ALL)]
    return projection(Plan(ALL, (2, -3, 3, "far"), far_rows, False, True), "project_rest", where,
                      acc, joined, j_first, j_second, j_far, ax2, a3, ax3, a4, ax4, lo_far, far_x)


def solution(mesh):
    grid = Mesh(mesh.devices.reshape(4, 8, 2, 4), ("y", "z", "c", "x"))
    tok = ("y", "z", "c")
    rows = P(tok, "x", None)
    placed = (rows, rows, rows, rows, P("x", None, tok), P("x", None, tok), P(), rows)
    return jax.shard_map(on_device, mesh=grid, in_specs=placed, out_specs=P(tok, "x"), check_vma=False)
```

```python
import jax
import jax.numpy as jnp
import numpy as np
from jax import lax
from jax.experimental import pallas as pl
from jax.experimental.pallas import tpu as pltpu
from jax.sharding import Mesh, PartitionSpec as P

SIZES = {"y": 4, "z": 8, "c": 2, "x": 4}
BLOCK = 128
MASKED = -1e30
ATTENTION_VMEM = 58 << 20
STRIP = 256
PROJECT_VMEM = 28 << 20
Y_FIRST = 512
LOG2E = 1.4426950408889634


def move(value, axes, target):
    axes = tuple(a for a in SIZES if a in axes)
    dims = [SIZES[a] for a in axes]
    pairs = []
    for source in range(int(np.prod(dims))):
        coords = dict(zip(axes, (int(v) for v in np.unravel_index(source, dims))))
        goal = target(**coords)
        goal = [goal[a] % SIZES[a] for a in axes]
        pairs.append((source, int(np.ravel_multi_index(goal, dims))))
    return lax.ppermute(value, axes, pairs)


def swap_cores(value):
    return move(value, ("c",), lambda c: dict(c=1 - c))


def along(value, axis, steps):
    sign = lambda c: steps if c == 0 else -steps
    return move(value, (axis, "c"), lambda c, **k: {axis: k[axis] + sign(c), "c": c})


def shift(value, axis, steps):
    return move(value, (axis,), lambda **k: {axis: k[axis] + steps})


def nt(a, b):
    return lax.dot_general(a, b, (((1,), (1,)), ((), ())), preferred_element_type=jnp.float32)


def nn(a, b):
    return jnp.dot(a, b, preferred_element_type=jnp.float32)


def attention_kernel(q_hbm, do_hbm, k_hbm, v_hbm, lse_hbm, delta_hbm, seg_ref, out_ref,
                     query_all, dout_all, k_ref, v_ref, lse_b, delta_b, bias, key_t, dk_acc, dv_acc, sems):
    heads, window, size = query_all.shape
    scale = size ** -0.5
    small = [pltpu.make_async_copy(source, target, sems.at[2 * heads + index]) for index, (source, target) in
             enumerate(((k_hbm, k_ref), (v_hbm, v_ref), (lse_hbm, lse_b), (delta_hbm, delta_b)))]
    for made in small:
        made.start()
    wide = []
    for head in range(heads):
        columns = slice(head * size, (head + 1) * size)
        wide.append([
            pltpu.make_async_copy(q_hbm.at[:, columns], query_all.at[head], sems.at[2 * head]),
            pltpu.make_async_copy(do_hbm.at[:, columns], dout_all.at[head], sems.at[2 * head + 1])])
        for made in wide[-1]:
            made.start()
    seg_row = seg_ref[...].astype(jnp.float32)
    seg_col = jnp.broadcast_to(seg_row, (BLOCK, window)).T
    row = lax.broadcasted_iota(jnp.int32, (window, BLOCK), 0)
    col = lax.broadcasted_iota(jnp.int32, (window, BLOCK), 1)
    for start in range(0, window, BLOCK):
        same = seg_col == seg_row[:, start:start + BLOCK]
        bias[:, start:start + BLOCK] = jnp.where(same & (row <= col + start), 0.0, MASKED)
    for made in small:
        made.wait()
    lse_f = lse_b[...].astype(jnp.float32) * LOG2E
    delta_f = delta_b[...].astype(jnp.float32)
    key_t[...] = k_ref[...].astype(jnp.float32).T.astype(jnp.bfloat16)
    for head in range(heads):
        for made in wide[head]:
            made.wait()
        lse = lse_f[head:head + 1, :]
        delta = delta_f[head:head + 1, :]
        for start in range(0, window, STRIP):
            rows = slice(start, start + STRIP)
            query = query_all[head, start:, :]
            dout = dout_all[head, start:, :]
            scores = nt(k_ref[rows, :], query)
            probs = jnp.exp2(scores * (scale * LOG2E) - lse[:, start:] + bias[rows, start:])
            grad_prob = nt(v_ref[rows, :], dout)
            grad_score = (probs * (grad_prob - delta[:, start:])).astype(jnp.bfloat16)
            dv = nn(probs.astype(jnp.bfloat16), dout)
            dk = nn(grad_score, query)
            part = nn(key_t[:, rows], grad_score)
            if head == 0:
                dv_acc[rows, :] = dv
                dk_acc[rows, :] = dk
            else:
                dv_acc[rows, :] += dv
                dk_acc[rows, :] += dk
            if start == 0:
                total = part
            else:
                total = jnp.concatenate([total[:, :start], total[:, start:] + part], axis=1)
        out_ref[:, head * size:(head + 1) * size] = (total * scale).T.astype(jnp.bfloat16)
    out_ref[:, heads * size:(heads + 1) * size] = (dk_acc[...] * scale).astype(jnp.bfloat16)
    out_ref[:, (heads + 1) * size:] = dv_acc[...].astype(jnp.bfloat16)


def joined_gradients(query, dout, key, value, lse, delta, seg):
    window, width = query.shape
    size = key.shape[1]
    heads = width // size
    hbm = pl.BlockSpec(memory_space=pltpu.HBM)
    vmem = pl.BlockSpec(memory_space=pltpu.VMEM)
    return pl.pallas_call(
        attention_kernel,
        in_specs=[hbm] * 6 + [vmem],
        out_specs=vmem,
        out_shape=jax.ShapeDtypeStruct((window, width + 2 * size), jnp.bfloat16),
        scratch_shapes=[
            pltpu.VMEM((heads, window, size), jnp.bfloat16),
            pltpu.VMEM((heads, window, size), jnp.bfloat16),
            pltpu.VMEM((window, size), jnp.bfloat16),
            pltpu.VMEM((window, size), jnp.bfloat16),
            pltpu.VMEM((heads, window), jnp.bfloat16),
            pltpu.VMEM((heads, window), jnp.bfloat16),
            pltpu.VMEM((window, window), jnp.float32),
            pltpu.VMEM((size, window), jnp.bfloat16),
            pltpu.VMEM((window, size), jnp.float32),
            pltpu.VMEM((window, size), jnp.float32),
            pltpu.SemaphoreType.DMA((2 * heads + 4,)),
        ],
        compiler_params=pltpu.CompilerParams(vmem_limit_bytes=ATTENTION_VMEM),
        cost_estimate=pl.CostEstimate(flops=4 * 10 ** 9, bytes_accessed=4 * 10 ** 6, transcendentals=10 ** 6),
        name="attention_backward",
    )(query, dout, key, value, lse, delta, seg)


def slot_offsets(c, part):
    sign = 1 - 2 * c
    first = 4 * c if part == "lo" else 4 - 4 * c
    step = -sign if part == "lo" else sign
    return [first] + [step * k for k in (1, 2, 3)]


class Plan:
    def __init__(self, joined, slots, rows, first, last):
        self.joined, self.slots, self.rows, self.first, self.last = joined, slots, rows, first, last


def projection_kernel(plan, where_ref, *refs):
    y, z, c, x = (where_ref[i] for i in range(4))
    sign = 1 - 2 * c
    refs = list(refs)
    acc_in = None if plan.first else refs.pop(0)
    heads = [refs.pop(0) for _ in plan.joined]
    slots = []
    for offset in plan.slots:
        slots.append([refs.pop(0), refs.pop(0)] if offset == "far" else [refs.pop(0)])
    rows = [refs.pop(0) for _ in plan.rows]
    out_ref, ja, jb, wa, far, wb, sems = refs[:7]
    acc = refs[7] if plan.last else out_ref
    split = Y_FIRST
    single = len(plan.joined) == 1
    one_row_head = len(plan.rows) == 2

    def steps(offset):
        return 2 if offset in (2, "far") else sign * offset

    def tile(offset):
        return (z + 8 + offset) % 8

    def head_index(head):
        return (x + steps(head) + 4) % 4

    used = [0]

    def copy(source, target):
        made = pltpu.make_async_copy(source, target, sems.at[used[0]])
        used[0] += 1
        return made

    def entry(offset, g):
        return ((y - g) * (sign if offset <= 0 else -sign) + 4) % 4

    ahead = [copy(source.at[:, :split], ja.at[index]) for index, source in enumerate(heads)]
    for index, (sources, offset) in enumerate(zip(slots, plan.slots)):
        if offset == "far":
            ahead += [copy(source, far.at[which]) for which, source in enumerate(sources)]
        elif single:
            ahead.append(copy(sources[0].at[entry(offset, head_index(plan.joined[0]))], wa.at[index, 0]))
        else:
            ahead.append(copy(sources[0], wa.at[index]))
    for made in ahead:
        made.start()

    meets = []
    for part, same, offset, against in plan.rows:
        g = (y + 4 + steps(offset)) % 4
        index = jnp.int32(-1)
        for position, head in enumerate(plan.joined):
            if head in against:
                index = jnp.where(head_index(head) == g, position, index)
        meets.append((g, index, len(against) == 4))

    def guarded(sure, index, body):
        body() if sure else pl.when(index >= 0)(body)

    row_heads = []
    if one_row_head:
        for position, source in enumerate(heads):
            made = pltpu.make_async_copy(source.at[:, split:], jb.at[0], sems.at[used[0]])
            pl.when(meets[0][1] == position)(made.start)
            row_heads.append(made)
        used[0] += 1
    else:
        row_heads = [copy(source.at[:, split:], jb.at[position]) for position, source in enumerate(heads)]
        for made in row_heads:
            made.start()
    row_copies = []
    for index, (source, (g, meet, sure)) in enumerate(zip(rows, meets)):
        made = copy(source, wb.at[index])
        guarded(sure, meet, made.start)
        row_copies.append(made)

    if plan.first:
        acc[...] = jnp.zeros_like(acc)
    else:
        acc[...] = acc_in[...]

    for made in ahead:
        made.wait()

    def slot(index, offset, g):
        if offset == "far":
            k = (y - g + 4) % 4
            from_zero = k < 2
            place = jnp.where(from_zero, k, (4 - k) % 4 - 1)
            return far[jnp.where(jnp.where(from_zero, 0, 1) == c, 0, 1), jnp.maximum(place, 0)]
        return wa[index, 0 if single else entry(offset, g)]

    for pair in range(0, len(slots), 2):
        total = None
        for position, head in enumerate(plan.joined):
            g = head_index(head)
            block = jnp.concatenate([slot(pair + k, plan.slots[pair + k], g) for k in range(2)], axis=0)
            term = nt(ja[position], block)
            total = term if total is None else total + term
        for k in range(2):
            offset = plan.slots[pair + k]
            acc[tile(4 if offset == "far" else sign * offset)] += total[:, k * BLOCK:(k + 1) * BLOCK]

    if one_row_head:
        pl.when(meets[0][1] >= 0)(row_heads[0].wait)
    else:
        for made in row_heads:
            made.wait()
    for index, ((part, same, offset, against), (g, meet, sure)) in enumerate(zip(plan.rows, meets)):
        offsets = slot_offsets(c if same else 1 - c, part)

        def body(index=index, meet=meet, offsets=offsets):
            row_copies[index].wait()
            left = jb[0] if one_row_head or single else jb[meet]
            for pair in (0, 2):
                term = nt(left, wb[index, pair:pair + 2].reshape(2 * BLOCK, wb.shape[3]))
                for k in range(2):
                    acc[tile(offsets[pair + k])] += term[:, k * BLOCK:(k + 1) * BLOCK]

        guarded(sure, meet, body)
    if plan.last:
        for place in range(8):
            out_ref[:, place * BLOCK:(place + 1) * BLOCK] = acc[place].astype(out_ref.dtype)


def projection(plan, name, where, *operands):
    window, width = operands[0 if plan.first else 1].shape
    columns = 8 * BLOCK
    vmem = pl.BlockSpec(memory_space=pltpu.VMEM)
    kept = 0 if plan.first else 1
    heads, slots, rows = len(plan.joined), len(plan.slots), len(plan.rows)
    share = (heads * slots + rows) / 40
    return pl.pallas_call(
        lambda *refs: projection_kernel(plan, *refs),
        in_specs=[pl.BlockSpec(memory_space=pltpu.SMEM)] + [vmem] * kept
        + [pl.BlockSpec(memory_space=pl.ANY)] * (len(operands) - kept),
        out_specs=vmem,
        out_shape=jax.ShapeDtypeStruct((window, columns), jnp.bfloat16) if plan.last
        else jax.ShapeDtypeStruct((8, window, BLOCK), jnp.float32),
        scratch_shapes=[
            pltpu.VMEM((heads, window, Y_FIRST), jnp.bfloat16),
            pltpu.VMEM((1 if rows == 2 else heads, window, width - Y_FIRST), jnp.bfloat16),
            pltpu.VMEM((slots, 1 if heads == 1 else 4, BLOCK, Y_FIRST), jnp.bfloat16),
            pltpu.VMEM((2, 2, BLOCK, Y_FIRST), jnp.bfloat16),
            pltpu.VMEM((rows, 4, BLOCK, width - Y_FIRST), jnp.bfloat16),
            pltpu.SemaphoreType.DMA((24,)),
        ] + [pltpu.VMEM((8, window, BLOCK), jnp.float32)] * plan.last,
        compiler_params=pltpu.CompilerParams(vmem_limit_bytes=PROJECT_VMEM),
        cost_estimate=pl.CostEstimate(
            flops=int(1e9 * share), bytes_accessed=int(1e6 * share), transcendentals=0),
        name=name,
    )(where, *operands)


ALL = (0, -1, 1, 2)
NEAR = (0, -1, 1)


def rows_of(against):
    return [("lo", True, 0, against), ("hi", True, 0, against), ("lo", True, -1, against),
            ("hi", True, -1, against), ("lo", False, 1, against), ("hi", False, 1, against)]


def far_rows(against):
    return [("lo", True, "far", against), ("lo", False, "far", against)]


def in_order(*values):
    return lax.optimization_barrier(values)


def on_device(query_rows, key_rows, value_rows, output_gradient, row_logsumexp, row_delta_sums,
              segments, query_key_value_weight):
    window, _, width = query_rows.shape
    place = [lax.axis_index(a) for a in ("y", "z", "c", "x")]
    core = place[2]
    where = jnp.stack(place).astype(jnp.int32)
    token_index = (place[0] * SIZES["z"] + place[1]) * SIZES["c"] + core

    weight = query_key_value_weight[:, 0]
    rows = weight.shape[0]
    turned = move(weight, ("y", "x"), lambda y, x: dict(y=x, x=y))

    seg = lax.dynamic_slice_in_dim(segments, token_index * window, window).reshape(1, window)
    joined = joined_gradients(
        query_rows.reshape(window, width), output_gradient.reshape(window, width),
        key_rows[:, 0], value_rows[:, 0], row_logsumexp[0], row_delta_sums[0], seg)
    j_first = along(joined, "x", 1)

    turned, joined, where = in_order(turned, joined, where)
    other = swap_cores(turned)
    j_second = along(joined, "x", -1)
    block = jnp.concatenate([jnp.where(core == 0, turned, other), jnp.where(core == 0, other, turned)], axis=0)
    a_block, b_block = in_order(block[:, :Y_FIRST], block[:, Y_FIRST:])
    own_half = lax.dynamic_slice_in_dim(b_block, core * rows, rows, 0)

    b1 = along(b_block, "z", 1)
    a_first = along(a_block, "y", 1)
    a_second = along(a_block, "y", -1)
    a_far = along(a_block, "y", 2)
    b4 = along(own_half, "z", 4)
    b23 = along(jnp.stack([b1, b_block]), "z", 2)
    a_own = jnp.stack([a_block, a_first, a_far, a_second])
    a1 = along(a_own, "z", 1)
    x1, x4, x23 = swap_cores(b1), swap_cores(b4), swap_cores(b23)
    far = jnp.concatenate([jnp.where(core == 0, b4, x4), jnp.where(core == 0, x4, b4)], axis=0)
    lo = jnp.stack([jnp.where(core == 0, b_block, far), b1, b23[1], b23[0]])
    hi = jnp.stack([jnp.where(core == 0, far, b_block), x1, x23[1], x23[0]])
    lo, hi = in_order(lo, hi)
    lo_next = along(lo, "y", 1)
    a2 = along(a1, "z", 1)
    ax1 = swap_cores(a1)
    hi_next = along(hi, "y", 1)
    lo_far = along(lo_next, "y", 1)
    a3 = along(a2, "z", 1)
    ax2 = swap_cores(a2)
    lo_x, hi_x = swap_cores(lo_next), swap_cores(hi_next)
    j_far = along(j_first, "x", 1)
    a4 = along(jnp.where(core == 0, a3[:2], a3[1:3]), "z", 1)

    ring = (a_own, a1, ax1, a2)
    near_rows = (lo, hi, lo_next, hi_next, lo_x, hi_x)
    acc = projection(Plan(NEAR, (0, -1, 1, -2), rows_of(NEAR), True, False), "project_near", where,
                     joined, j_first, j_second, *ring, *near_rows)
    acc, lo_far, a4 = in_order(acc, lo_far, a4)
    far_x = swap_cores(lo_far)
    ax3 = swap_cores(a3)
    ax4 = swap_cores(a4)
    rest = (ax2, a3, ax3, a4, ax4)
    acc = projection(Plan(NEAR, (2, -3, 3, "far"), far_rows(NEAR), False, False), "project_rest", where,
                     acc, joined, j_first, j_second, *rest, lo_far, far_x)
    acc, j_far = in_order(acc, j_far)
    plan = Plan((2,), (0, -1, 1, -2, 2, -3, 3, "far"), rows_of((2,)) + far_rows((2,)), False, True)
    return projection(plan, "project_far_head", where, acc, j_far, *ring, *rest, *near_rows, lo_far, far_x)


def solution(mesh):
    grid = Mesh(mesh.devices.reshape(4, 8, 2, 4), ("y", "z", "c", "x"))
    tok = ("y", "z", "c")
    rows = P(tok, "x", None)
    placed = (rows, rows, rows, rows, P("x", None, tok), P("x", None, tok), P(), rows)
    return jax.shard_map(on_device, mesh=grid, in_specs=placed, out_specs=P(tok, "x"), check_vma=False)
```

```python
import jax
import jax.numpy as jnp
import numpy as np
from jax import lax
from jax.experimental import pallas as pl
from jax.experimental.pallas import tpu as pltpu
from jax.sharding import Mesh, PartitionSpec as P

SIZES = {"y": 4, "z": 8, "c": 2, "x": 4}
BLOCK = 128
MASKED = -1e30
ATTENTION_VMEM = 58 << 20
STRIP = 256
PROJECT_VMEM = 28 << 20
Y_FIRST = 512
LOG2E = 1.4426950408889634


def move(value, axes, target):
    axes = tuple(a for a in SIZES if a in axes)
    dims = [SIZES[a] for a in axes]
    pairs = []
    for source in range(int(np.prod(dims))):
        coords = dict(zip(axes, (int(v) for v in np.unravel_index(source, dims))))
        goal = target(**coords)
        goal = [goal[a] % SIZES[a] for a in axes]
        pairs.append((source, int(np.ravel_multi_index(goal, dims))))
    return lax.ppermute(value, axes, pairs)


def swap_cores(value):
    return move(value, ("c",), lambda c: dict(c=1 - c))


def along(value, axis, steps):
    sign = lambda c: steps if c == 0 else -steps
    return move(value, (axis, "c"), lambda c, **k: {axis: k[axis] + sign(c), "c": c})


def shift(value, axis, steps):
    return move(value, (axis,), lambda **k: {axis: k[axis] + steps})


def nt(a, b):
    return lax.dot_general(a, b, (((1,), (1,)), ((), ())), preferred_element_type=jnp.float32)


def nn(a, b):
    return jnp.dot(a, b, preferred_element_type=jnp.float32)


def attention_kernel(q_hbm, do_hbm, k_hbm, v_hbm, lse_hbm, delta_hbm, seg_ref, out_ref,
                     query_all, dout_all, k_ref, v_ref, lse_b, delta_b, bias, key_t, dk_acc, dv_acc, sems):
    heads, window, size = query_all.shape
    scale = size ** -0.5
    small = [pltpu.make_async_copy(source, target, sems.at[2 * heads + index]) for index, (source, target) in
             enumerate(((k_hbm, k_ref), (v_hbm, v_ref), (lse_hbm, lse_b), (delta_hbm, delta_b)))]
    for made in small:
        made.start()
    wide = []
    for head in range(heads):
        columns = slice(head * size, (head + 1) * size)
        wide.append([
            pltpu.make_async_copy(q_hbm.at[:, columns], query_all.at[head], sems.at[2 * head]),
            pltpu.make_async_copy(do_hbm.at[:, columns], dout_all.at[head], sems.at[2 * head + 1])])
        for made in wide[-1]:
            made.start()
    seg_row = seg_ref[...].astype(jnp.float32)
    seg_col = jnp.broadcast_to(seg_row, (BLOCK, window)).T
    row = lax.broadcasted_iota(jnp.int32, (window, BLOCK), 0)
    col = lax.broadcasted_iota(jnp.int32, (window, BLOCK), 1)
    for start in range(0, window, BLOCK):
        same = seg_col == seg_row[:, start:start + BLOCK]
        bias[:, start:start + BLOCK] = jnp.where(same & (row <= col + start), 0.0, MASKED)
    for made in small:
        made.wait()
    lse_f = lse_b[...].astype(jnp.float32) * LOG2E
    delta_f = delta_b[...].astype(jnp.float32)
    key_t[...] = k_ref[...].astype(jnp.float32).T.astype(jnp.bfloat16)
    for head in range(heads):
        for made in wide[head]:
            made.wait()
        lse = lse_f[head:head + 1, :]
        delta = delta_f[head:head + 1, :]
        for start in range(0, window, STRIP):
            rows = slice(start, start + STRIP)
            query = query_all[head, start:, :]
            dout = dout_all[head, start:, :]
            scores = nt(k_ref[rows, :], query)
            probs = jnp.exp2(scores * (scale * LOG2E) - lse[:, start:] + bias[rows, start:])
            grad_prob = nt(v_ref[rows, :], dout)
            grad_score = (probs * (grad_prob - delta[:, start:])).astype(jnp.bfloat16)
            dv = nn(probs.astype(jnp.bfloat16), dout)
            dk = nn(grad_score, query)
            part = nn(key_t[:, rows], grad_score)
            if head == 0:
                dv_acc[rows, :] = dv
                dk_acc[rows, :] = dk
            else:
                dv_acc[rows, :] += dv
                dk_acc[rows, :] += dk
            if start == 0:
                total = part
            else:
                total = jnp.concatenate([total[:, :start], total[:, start:] + part], axis=1)
        out_ref[:, head * size:(head + 1) * size] = (total * scale).T.astype(jnp.bfloat16)
    out_ref[:, heads * size:(heads + 1) * size] = (dk_acc[...] * scale).astype(jnp.bfloat16)
    out_ref[:, (heads + 1) * size:] = dv_acc[...].astype(jnp.bfloat16)


def joined_gradients(query, dout, key, value, lse, delta, seg):
    window, width = query.shape
    size = key.shape[1]
    heads = width // size
    hbm = pl.BlockSpec(memory_space=pltpu.HBM)
    vmem = pl.BlockSpec(memory_space=pltpu.VMEM)
    return pl.pallas_call(
        attention_kernel,
        in_specs=[hbm] * 6 + [vmem],
        out_specs=vmem,
        out_shape=jax.ShapeDtypeStruct((window, width + 2 * size), jnp.bfloat16),
        scratch_shapes=[
            pltpu.VMEM((heads, window, size), jnp.bfloat16),
            pltpu.VMEM((heads, window, size), jnp.bfloat16),
            pltpu.VMEM((window, size), jnp.bfloat16),
            pltpu.VMEM((window, size), jnp.bfloat16),
            pltpu.VMEM((heads, window), jnp.bfloat16),
            pltpu.VMEM((heads, window), jnp.bfloat16),
            pltpu.VMEM((window, window), jnp.float32),
            pltpu.VMEM((size, window), jnp.bfloat16),
            pltpu.VMEM((window, size), jnp.float32),
            pltpu.VMEM((window, size), jnp.float32),
            pltpu.SemaphoreType.DMA((2 * heads + 4,)),
        ],
        compiler_params=pltpu.CompilerParams(vmem_limit_bytes=ATTENTION_VMEM),
        cost_estimate=pl.CostEstimate(flops=4 * 10 ** 9, bytes_accessed=4 * 10 ** 6, transcendentals=10 ** 6),
        name="attention_backward",
    )(query, dout, key, value, lse, delta, seg)


def slot_offsets(c, part):
    sign = 1 - 2 * c
    first = 4 * c if part == "lo" else 4 - 4 * c
    step = -sign if part == "lo" else sign
    return [first] + [step * k for k in (1, 2, 3)]


class Plan:
    def __init__(self, joined, slots, rows, first, last):
        self.joined, self.slots, self.rows, self.first, self.last = joined, slots, rows, first, last


def projection_kernel(plan, where_ref, *refs):
    y, z, c, x = (where_ref[i] for i in range(4))
    sign = 1 - 2 * c
    refs = list(refs)
    acc_in = None if plan.first else refs.pop(0)
    heads = [refs.pop(0) for _ in plan.joined]
    slots = []
    for offset in plan.slots:
        slots.append([refs.pop(0), refs.pop(0)] if offset == "far" else [refs.pop(0)])
    rows = [refs.pop(0) for _ in plan.rows]
    out_ref, jb = refs[:2]
    acc = refs[2] if plan.last else out_ref
    width = heads[0].shape[1]
    split = Y_FIRST
    single = len(plan.joined) == 1
    one_row_head = len(plan.rows) == 2

    def steps(offset):
        return 2 if offset in (2, "far") else sign * offset

    def tile(offset):
        return (z + 8 + offset) % 8

    def head_index(head):
        return (x + steps(head) + 4) % 4

    def entry(offset, g):
        return ((y - g) * (sign if offset <= 0 else -sign) + 4) % 4

    meets = []
    for part, same, offset, against in plan.rows:
        g = (y + 4 + steps(offset)) % 4
        index = jnp.int32(-1)
        for position, head in enumerate(plan.joined):
            if head in against:
                index = jnp.where(head_index(head) == g, position, index)
        meets.append((g, index, len(against) == 4))

    def guarded(sure, index, body):
        body() if sure else pl.when(index >= 0)(body)

    if not single:
        for position, source in enumerate(heads):
            if one_row_head:

                @pl.when(meets[0][1] == position)
                def _(source=source):
                    jb[0] = source[:, split:]
            else:
                jb[position] = source[:, split:]

    if plan.first:
        acc[...] = jnp.zeros_like(acc)
    else:
        acc[...] = acc_in[...]

    def slot(index, offset, g):
        if offset == "far":
            k = (y - g + 4) % 4
            from_zero = k < 2
            place = jnp.where(from_zero, k, (4 - k) % 4 - 1)
            place = jnp.maximum(place, 0)
            here = jnp.where(from_zero, 0, 1) == c
            return jnp.where(here, slots[index][0][place], slots[index][1][place])
        return slots[index][0][entry(offset, g)]

    for pair in range(0, len(slots), 2):
        total = None
        for position, head in enumerate(plan.joined):
            g = head_index(head)
            block = jnp.concatenate([slot(pair + k, plan.slots[pair + k], g) for k in range(2)], axis=0)
            term = nt(heads[position][:, :split], block)
            total = term if total is None else total + term
        for k in range(2):
            offset = plan.slots[pair + k]
            acc[tile(4 if offset == "far" else sign * offset)] += total[:, k * BLOCK:(k + 1) * BLOCK]

    for index, ((part, same, offset, against), (g, meet, sure)) in enumerate(zip(plan.rows, meets)):
        offsets = slot_offsets(c if same else 1 - c, part)

        def body(index=index, meet=meet, offsets=offsets):
            left = heads[0][:, split:] if single else jb[0] if one_row_head else jb[meet]
            for pair in (0, 2):
                term = nt(left, rows[index][pair:pair + 2].reshape(2 * BLOCK, width - split))
                for k in range(2):
                    acc[tile(offsets[pair + k])] += term[:, k * BLOCK:(k + 1) * BLOCK]

        guarded(sure, meet, body)
    if plan.last:
        for place in range(8):
            out_ref[:, place * BLOCK:(place + 1) * BLOCK] = acc[place].astype(out_ref.dtype)


def projection(plan, name, where, *operands):
    window, width = operands[0 if plan.first else 1].shape
    columns = 8 * BLOCK
    vmem = pl.BlockSpec(memory_space=pltpu.VMEM)
    kept = 0 if plan.first else 1
    heads, slots, rows = len(plan.joined), len(plan.slots), len(plan.rows)
    share = (heads * slots + rows) / 40
    return pl.pallas_call(
        lambda *refs: projection_kernel(plan, *refs),
        in_specs=[pl.BlockSpec(memory_space=pltpu.SMEM)] + [vmem] * len(operands),
        out_specs=vmem,
        out_shape=jax.ShapeDtypeStruct((window, columns), jnp.bfloat16) if plan.last
        else jax.ShapeDtypeStruct((8, window, BLOCK), jnp.float32),
        scratch_shapes=[
            pltpu.VMEM((1 if rows == 2 else heads, window, width - Y_FIRST), jnp.bfloat16),
        ] + [pltpu.VMEM((8, window, BLOCK), jnp.float32)] * plan.last,
        compiler_params=pltpu.CompilerParams(vmem_limit_bytes=PROJECT_VMEM),
        cost_estimate=pl.CostEstimate(
            flops=int(1e9 * share), bytes_accessed=int(1e6 * share), transcendentals=0),
        name=name,
    )(where, *operands)


ALL = (0, -1, 1, 2)
NEAR = (0, -1, 1)


def rows_of(against):
    return [("lo", True, 0, against), ("hi", True, 0, against), ("lo", True, -1, against),
            ("hi", True, -1, against), ("lo", False, 1, against), ("hi", False, 1, against)]


def far_rows(against):
    return [("lo", True, "far", against), ("lo", False, "far", against)]


def in_order(*values):
    return lax.optimization_barrier(values)


def on_device(query_rows, key_rows, value_rows, output_gradient, row_logsumexp, row_delta_sums,
              segments, query_key_value_weight):
    window, _, width = query_rows.shape
    place = [lax.axis_index(a) for a in ("y", "z", "c", "x")]
    core = place[2]
    where = jnp.stack(place).astype(jnp.int32)
    token_index = (place[0] * SIZES["z"] + place[1]) * SIZES["c"] + core

    weight = query_key_value_weight[:, 0]
    rows = weight.shape[0]
    turned = move(weight, ("y", "x"), lambda y, x: dict(y=x, x=y))

    seg = lax.dynamic_slice_in_dim(segments, token_index * window, window).reshape(1, window)
    joined = joined_gradients(
        query_rows.reshape(window, width), output_gradient.reshape(window, width),
        key_rows[:, 0], value_rows[:, 0], row_logsumexp[0], row_delta_sums[0], seg)
    j_first = along(joined, "x", 1)

    turned, joined, where = in_order(turned, joined, where)
    other = swap_cores(turned)
    j_second = along(joined, "x", -1)
    block = jnp.concatenate([jnp.where(core == 0, turned, other), jnp.where(core == 0, other, turned)], axis=0)
    a_block, b_block = in_order(block[:, :Y_FIRST], block[:, Y_FIRST:])
    own_half = lax.dynamic_slice_in_dim(b_block, core * rows, rows, 0)

    b1 = along(b_block, "z", 1)
    a_first = along(a_block, "y", 1)
    a_second = along(a_block, "y", -1)
    a_far = along(a_block, "y", 2)
    b4 = along(own_half, "z", 4)
    b23 = along(jnp.stack([b1, b_block]), "z", 2)
    a_own = jnp.stack([a_block, a_first, a_far, a_second])
    a1 = along(a_own, "z", 1)
    x1, x4, x23 = swap_cores(b1), swap_cores(b4), swap_cores(b23)
    far = jnp.concatenate([jnp.where(core == 0, b4, x4), jnp.where(core == 0, x4, b4)], axis=0)
    lo = jnp.stack([jnp.where(core == 0, b_block, far), b1, b23[1], b23[0]])
    hi = jnp.stack([jnp.where(core == 0, far, b_block), x1, x23[1], x23[0]])
    lo, hi = in_order(lo, hi)
    lo_next = along(lo, "y", 1)
    a2 = along(a1, "z", 1)
    ax1 = swap_cores(a1)
    hi_next = along(hi, "y", 1)
    lo_far = along(lo_next, "y", 1)
    a3 = along(a2, "z", 1)
    ax2 = swap_cores(a2)
    lo_x, hi_x = swap_cores(lo_next), swap_cores(hi_next)
    j_far = along(j_first, "x", 1)
    a4 = along(jnp.where(core == 0, a3[:2], a3[1:3]), "z", 1)

    ring = (a_own, a1, ax1, a2)
    near_rows = (lo, hi, lo_next, hi_next, lo_x, hi_x)
    acc = projection(Plan(NEAR, (0, -1, 1, -2), rows_of(NEAR), True, False), "project_near", where,
                     joined, j_first, j_second, *ring, *near_rows)
    acc, lo_far, a4 = in_order(acc, lo_far, a4)
    far_x = swap_cores(lo_far)
    ax3 = swap_cores(a3)
    ax4 = swap_cores(a4)
    rest = (ax2, a3, ax3, a4, ax4)
    acc = projection(Plan(NEAR, (2, -3, 3, "far"), far_rows(NEAR), False, False), "project_rest", where,
                     acc, joined, j_first, j_second, *rest, lo_far, far_x)
    acc, j_far = in_order(acc, j_far)
    plan = Plan((2,), (0, -1, 1, -2, 2, -3, 3, "far"), rows_of((2,)) + far_rows((2,)), False, True)
    return projection(plan, "project_far_head", where, acc, j_far, *ring, *rest, *near_rows, lo_far, far_x)


def solution(mesh):
    grid = Mesh(mesh.devices.reshape(4, 8, 2, 4), ("y", "z", "c", "x"))
    tok = ("y", "z", "c")
    rows = P(tok, "x", None)
    placed = (rows, rows, rows, rows, P("x", None, tok), P("x", None, tok), P(), rows)
    return jax.shard_map(on_device, mesh=grid, in_specs=placed, out_specs=P(tok, "x"), check_vma=False)
```
